32 devices in a mesh: blk: 16 (over z, y, core), rep: 2 (over x).
Axes of the slice: x: 2, y: 2, z: 4, core: 2. Of those that a mesh axis runs over, the one named last changes fastest.
Arguments:
- factors: float32 [16, 2, 300, 512], P('blk', None, 'rep'), may hold values from -1.5 to 1.5
- state: float32 [16, 2, 300, 512], P('blk', None, 'rep'), may hold values from 30 to 3000
- counts: int32 [16, 8, 512, 512], P('blk'), may hold values from 0 to 1024, as said below
Outputs:
- step: float32 [16, 2, 300, 512], P('blk', None, 'rep')
- new_state: float32 [16, 2, 300, 512], P('blk', None, 'rep')
The draws below stay inside these ranges and needn't reach their ends.
Inputs may be any that keep to these rules, and one draw needn't show every extreme that they name: counts[p, r] is the tile of the two blocks that meet at player p in round r, and each pair of blocks meets at most once in the 8 rounds.
All inputs are finite; a program needn't handle non-finite values.
Results may differ from the reference program's by a relative error of at most 0.0003.
Values sent between devices are 32-bit elements; how exact they have to be, the bound alone decides.
No kernel may reach another device: no remote copies, remote signals or barrier semaphores. Data moves between devices by JAX's collectives and lax.ppermute only.
A program may use at most 128 MiB of HBM per device.

```python
import math
import jax
import jax.numpy as jnp
from jax import lax

B = 512
D = 300
ROUNDS = 8
PLAYERS = 16


def draw_counts(key, part):
    first, second, third = jax.random.split(jax.random.fold_in(key, 17), 3)
    shape = (PLAYERS, ROUNDS, B, B)
    mantissa = jax.random.randint(first, shape, 0, 1024)
    shifted = jax.random.randint(second, shape, 0, 10)
    present = jax.random.randint(third, shape, 0, 3)
    value = 1 + jnp.right_shift(mantissa, shifted)
    return jnp.where(present == 0, 0, value).astype(jnp.int32)


def block_scale(stream_key, dims, shards, low, high):
    gain, own = 1.0, jax.random.fold_in(stream_key, 6)
    for axis_at, blocks in shards:
        heights = jnp.exp(jax.random.uniform(jax.random.fold_in(own, axis_at), (blocks,), jnp.float32, low / len(shards), high / len(shards)))
        gain = gain * jnp.repeat(heights, dims[axis_at] // blocks).reshape([-1 if axis == axis_at else 1 for axis in range(len(dims))])
    return gain


def normal_values(own_key, dims, scale, most, cuts=(), kind=jnp.bfloat16):
    result = jax.random.normal(own_key, dims, jnp.float32) * scale
    if len(cuts) > 0:
        result = block_scale(own_key, dims, cuts, -0.22, 0.18) * result
    return jnp.clip(result, min=-most, max=most).astype(kind)


def setup_inputs(seed: int = 0) -> dict:
    keys = jax.random.split(jax.random.key(seed), 4)
    factors = normal_values(keys[0], (PLAYERS, 2, D, B), 0.25, 1.5, ((0, 16), (2, 2)), jnp.float32)
    state = jnp.clip(jnp.exp(math.log(3000.0) - 4.6051702 * jax.random.uniform(keys[1], (PLAYERS, 2, D, B), jnp.float32) ** block_scale(keys[1], (PLAYERS, 2, D, B), ((0, 16), (2, 2)), -0.2, 0.2)), 30.0, 3000.0)
    counts = draw_counts(jax.random.fold_in(keys[3], 71), 0)
    return {"factors": factors, "state": state, "counts": counts}


clip_bound = 2.0

def residual_of(scores, count_tile):
    amount = count_tile.astype(jnp.float32)
    present = count_tile > 0
    clamped = jnp.maximum(amount, 1.0)
    weight = 0.1 + 0.25 * jnp.sqrt(clamped)
    kept = weight * jnp.clip(scores - jnp.log(clamped), -clip_bound, clip_bound)
    return jnp.where(present, kept, 0.5 * jax.nn.sigmoid(scores))

def meeting(operands):
    upper_block, lower_block, count_tile = operands
    scores = jnp.dot(upper_block.T, lower_block, precision=lax.Precision.HIGHEST, preferred_element_type=jnp.float32)
    residual = residual_of(scores, count_tile)
    grad_upper = jnp.dot(lower_block, residual.T, precision=lax.Precision.HIGHEST, preferred_element_type=jnp.float32)
    grad_lower = jnp.dot(upper_block, residual, precision=lax.Precision.HIGHEST, preferred_element_type=jnp.float32)
    return (grad_upper, grad_lower)

def rotate(upper, lower):
    players = upper.shape[0]
    new_upper = jnp.concatenate([upper[:1], lower[:1], upper[1:players - 1]], axis=0)
    new_lower = jnp.concatenate([lower[1:], upper[players - 1:]], axis=0)
    return (new_upper, new_lower)

def rotate_back(upper, lower):
    players = upper.shape[0]
    old_upper = jnp.concatenate([upper[:1], upper[2:], lower[players - 1:]], axis=0)
    old_lower = jnp.concatenate([upper[1:2], lower[:players - 1]], axis=0)
    return (old_upper, old_lower)

def reference(factors, state, counts):
    upper = factors[:, 0]
    lower = factors[:, 1]
    acc_upper = jnp.zeros_like(upper)
    acc_lower = jnp.zeros_like(lower)
    for turn in range(ROUNDS):
        grad_upper, grad_lower = lax.map(meeting, (upper, lower, counts[:, turn]))
        acc_upper = acc_upper + grad_upper
        acc_lower = acc_lower + grad_lower
        if turn < ROUNDS - 1:
            upper, lower = rotate(upper, lower)
            acc_upper, acc_lower = rotate(acc_upper, acc_lower)
    for turn in range(ROUNDS - 1):
        acc_upper, acc_lower = rotate_back(acc_upper, acc_lower)
    grad = jnp.stack([acc_upper, acc_lower], axis=1)
    new_state = state + grad * grad
    step = grad / jnp.sqrt(new_state)
    return (step, new_state)
```

```python
import functools
import jax
import jax.numpy as jnp
from jax import lax
from jax.experimental import pallas as pl
from jax.experimental.pallas import tpu as pltpu
from jax.sharding import PartitionSpec as P

clip_bound = 2.0
AXES = ("blk", "rep")


def place(row, side, core, plane):
    return ((2 * row + side) * 2 + core) * 2 + plane


def routes(rows):
    own = [(r, s, c, x) for r in range(rows) for s in range(2) for c in range(2) for x in range(2)]
    gather = [(place(r, s, c, x), place(r, s, x, c)) for r, s, c, x in own]
    cores = [(place(r, s, c, x), place(r, s, 1 - c, x)) for r, s, c, x in own]
    near, far, side, late = [], [], [], []
    for r, s, c, x in own:
        me = place(r, s, c, x)
        if c == 0:
            to = place(r + 1, s, 0, x) if r < rows - 1 else place(r, 1 - s, 1, 1 - x)
            near.append((me, to))
            far.append((me, to))
        elif r > 0:
            to = place(r - 1, s, 1, x)
            near.append((me, to))
            far.append((me, to))
        elif x == 1:
            to = place(0, 1 - s, 0, 1)
            near.append((me, to))
            far.append((me, to))
        else:
            if s == 1:
                near.append((me, place(0, 1, 0, 0)))
                far.append((me, place(0, 1, 0, 0)))
        side.append((me, place(r, 1 - s, c, x)))
    first = [(place(r, s, c, x), place(r, 1 - s, c, x)) for r, s, c, x in own if c == s]
    first.append((place(0, 0, 1, 0), place(0, 0, 0, 1)))
    first.append((place(1, 0, 1, 0), place(0, 0, 0, 0)))
    late = [(place(r, s, c, x), place(r, 1 - s, c, x)) for r, s, c, x in own if c != s]
    return dict(gather=gather, cores=cores, near=near, far=far, side=side, first=first, late=late)


def send(block, pairs):
    return lax.ppermute(block, AXES, pairs)


def back(pairs):
    return [(b, a) for a, b in pairs]


def residual_of(scores, count_tile):
    amount = count_tile.astype(jnp.float32)
    present = count_tile > 0
    clamped = jnp.maximum(amount, 1.0)
    weight = 0.1 + 0.25 * jnp.sqrt(clamped)
    kept = weight * jnp.clip(scores - jnp.log(clamped), -clip_bound, clip_bound)
    return jnp.where(present, kept, 0.5 / (1.0 + jnp.exp(-scores)))


def split(value):
    high = value.astype(jnp.bfloat16)
    return high, (value - high.astype(jnp.float32)).astype(jnp.bfloat16)


def dot(left, right, dims):
    return lax.dot_general(left, right, (dims, ((), ())), preferred_element_type=jnp.float32)


ACTIVE, MAIN, OTHER, TILE, SWAP, CORE, OUT_MAIN, OUT_OTHER, ZERO = range(9)


def meet_kernel(meetings, n_blocks, n_out, n_kept, cfg, counts, *refs):
    blocks = refs[:n_blocks]
    outs = refs[n_blocks + n_kept : n_blocks + n_kept + n_out]
    tile, raw, high, low, res_high, res_low, grad, sems, out_sems = refs[n_blocks + n_kept + n_out :]
    half = raw.shape[2]
    size = tile.shape[0]
    pad = high.shape[2]
    high[:, :, half - half % 16 : pad, :] = jnp.zeros((2, 2, pad - (half - half % 16), size), jnp.bfloat16)
    low[:, :, half - half % 16 : pad, :] = jnp.zeros((2, 2, pad - (half - half % 16), size), jnp.bfloat16)
    for q in range(meetings):

        @pl.when(cfg[q, ACTIVE] == 1)
        def _():
            pltpu.make_async_copy(counts.at[cfg[q, TILE]], tile, sems.at[2]).start()
            for b in range(n_blocks):
                for which, column in ((0, MAIN), (1, OTHER)):

                    @pl.when(cfg[q, column] == b)
                    def _():
                        pltpu.make_async_copy(blocks[b], raw.at[which], sems.at[which]).start()

            core = cfg[q, CORE]
            for which in range(2):
                pltpu.make_async_copy(blocks[0], raw.at[which], sems.at[which]).wait()
                for h in range(2):
                    to = h if which == 0 else jnp.where(cfg[q, SWAP] == 1, 1 - h, h)
                    hi, lo = split(raw[which, h])
                    high[which, to, 0:half, :] = hi
                    low[which, to, 0:half, :] = lo
            pltpu.make_async_copy(counts.at[0], tile, sems.at[2]).wait()
            up_h = high[core].reshape(2 * pad, size)
            up_l = low[core].reshape(2 * pad, size)
            lo_h = high[1 - core].reshape(2 * pad, size)
            lo_l = low[1 - core].reshape(2 * pad, size)
            right = jnp.concatenate([lo_h, lo_l, lo_h], axis=0)
            left = jnp.concatenate([up_h, up_h, up_l], axis=0)
            rows = min(size, 256)
            for s in range(size // rows):
                band = slice(s * rows, (s + 1) * rows)
                scores = dot(left[:, band], right, ((0,), (0,)))
                hi, lo = split(residual_of(scores, tile[band, :]))
                res_high[band, :] = hi
                res_low[band, :] = lo
            rh = res_high[...]
            rl = res_low[...]
            across = ((1,), (1,))
            along = ((1,), (0,))
            grad_upper = dot(lo_h, rh, across) + dot(lo_l, rh, across) + dot(lo_h, rl, across)
            grad_lower = dot(up_h, rh, along) + dot(up_l, rh, along) + dot(up_h, rl, along)
            for h in range(2):
                band = slice(h * pad, h * pad + half)
                for which, value in ((0, grad_upper), (1, grad_lower)):
                    target = jnp.where(core == 0, which, 1 - which)
                    to = jnp.where((cfg[q, SWAP] == 1) & (target == 1), 1 - h, h)
                    grad[target, to] = value[band, :]
            for o in range(n_out):
                for which, column in ((0, OUT_MAIN), (1, OUT_OTHER)):

                    @pl.when(cfg[q, column] == o)
                    def _():
                        pltpu.make_async_copy(grad.at[which], outs[o], out_sems.at[which]).start()

            for which in range(2):
                pltpu.make_async_copy(grad.at[which], outs[0], out_sems.at[which]).wait()

        @pl.when(cfg[q, ZERO] >= 0)
        def _():
            grad[0] = jnp.zeros(grad.shape[1:], jnp.float32)
            for o in range(n_out):

                @pl.when(cfg[q, ZERO] == o)
                def _():
                    copy = pltpu.make_async_copy(grad.at[0], outs[o], out_sems.at[0])
                    copy.start()
                    copy.wait()


def meet(cfg, counts, blocks, kept, fresh):
    meetings = cfg.shape[0]
    _, half, size = blocks[0].shape
    pad = -(-half // 16) * 16
    n_out = len(kept) + fresh
    shape = jax.ShapeDtypeStruct(blocks[0].shape, jnp.float32)
    hbm = pl.BlockSpec(memory_space=pl.ANY)
    return pl.pallas_call(
        functools.partial(meet_kernel, meetings, len(blocks), n_out, len(kept)),
        out_shape=[shape] * n_out,
        in_specs=[pl.BlockSpec(memory_space=pltpu.SMEM)] + [hbm] * (1 + len(blocks) + len(kept)),
        out_specs=[hbm] * n_out,
        input_output_aliases={2 + len(blocks) + i: i for i in range(len(kept))},
        scratch_shapes=[
            pltpu.VMEM((size, size), jnp.int32),
            pltpu.VMEM((2, 2, half, size), jnp.float32),
            pltpu.VMEM((2, 2, pad, size), jnp.bfloat16),
            pltpu.VMEM((2, 2, pad, size), jnp.bfloat16),
            pltpu.VMEM((size, size), jnp.bfloat16),
            pltpu.VMEM((size, size), jnp.bfloat16),
            pltpu.VMEM((2, 2, half, size), jnp.float32),
            pltpu.SemaphoreType.DMA((3,)),
            pltpu.SemaphoreType.DMA((2,)),
        ],
        cost_estimate=pl.CostEstimate(
            flops=meetings * 18 * half * 2 * size * size,
            bytes_accessed=meetings * (4 * size * size + 32 * half * size),
            transcendentals=meetings * 3 * size * size,
        ),
    )(cfg, counts, *blocks, *kept)


def body(factors, state, counts):
    players = lax.axis_size("blk")
    chips = players // 2
    way = routes(chips // 2)
    player = lax.axis_index("blk")
    x = lax.axis_index("rep")
    chip, c = player // 2, player % 2
    y = chip % 2
    tiles = counts[0]

    def at(player_, plane):
        return (player == player_) & (x == plane)

    native = c == x
    inner = c == y
    origin = (chip == 0) & (x == 0)

    def pick(cond, one, two):
        return jnp.where(cond, one, two)

    mine = send(factors[0], way["gather"])
    theirs = send(mine, way["cores"])
    first_upper = pick(origin, 1, 0)
    main_at = pick(c == 0, first_upper, 1)
    other_at = pick(c == 0, 1, first_upper)

    def take(stack, i):
        return lax.dynamic_index_in_dim(stack, i, 0, keepdims=False)

    main0 = jnp.stack([take(mine, main_at), take(theirs, main_at)])
    other0 = jnp.stack([take(theirs, other_at), take(mine, other_at)])
    head = pick(c == 0, jnp.stack([mine[0], theirs[0]]), jnp.stack([theirs[0], mine[0]]))
    got_first = send(pick(at(1, 0), head, main0), way["first"])
    got_near = send(main0, way["near"])
    main2 = pick(at(0, 0), got_first, got_near)
    got_side = send(main2, way["side"])
    main4 = send(main2, way["far"])
    got_late = send(main4, way["late"])
    other_first = send(got_first, way["cores"])
    other2 = send(main2, way["cores"])
    other_side = send(got_side, way["cores"])
    other_late = send(got_late, way["cores"])

    leader = player == 0
    up_skip = pick((c == 0) & ~native, 1, 0)
    low_skip = pick((c == 1) & ~native, 1, 0)

    def row(active, main, other, k, out_main, out_other, zero):
        turned_up = (chip - (k + up_skip) < 0) & ~leader
        turned_low = chip + k + low_skip >= chips
        swap = turned_up == turned_low
        tile = 2 * k + pick(native, 0, 1)
        values = [active, main, other, tile, swap, c, out_main, out_other, zero]
        return jnp.stack([jnp.asarray(v).astype(jnp.int32) for v in values])

    no = -1
    cfg = jnp.stack([row(native, pick(leader, 2, 0), 1, 0, 0, 1, pick(native, no, 0))])
    grad0, to_other0 = meet(cfg, tiles, [main0, other0, head], [], 2)
    cfg = jnp.stack([row(native, pick(leader, 2, 0), 1, 2, 0, 1, no)])
    grad2, to_other2 = meet(cfg, tiles, [main2, other2, head], [], 2)

    def lead(index):
        return pick(leader, pick(x == 0, 0, 1), index)

    main1 = lead(pick(inner, 2, 1))
    other1 = pick(inner, 4, 5)
    cfg = jnp.stack(
        [
            row(True, main1, pick(native, other1, 6), pick(native, 1, 0), 2, pick(native, 3, 0), no),
            row(~native, lead(3), other1, 1, 1, 3, no),
        ]
    )
    blocks = [head, got_first, got_side, main2, other_first, other_side, other0]
    to_other0, grad2, grad1, to_other1 = meet(cfg, tiles, blocks, [to_other0, grad2], 2)
    main3 = lead(pick(inner, 3, 2))
    other3 = pick(inner, 6, 7)
    cfg = jnp.stack(
        [
            row(True, main3, pick(native, other3, 5), pick(native, 3, 2), 1, pick(native, 3, 0), no),
            row(~native, lead(4), other3, 3, 2, 3, pick(native, 2, no)),
        ]
    )
    blocks = [head, got_first, got_side, got_late, main4, other2, other_side, other_late]
    to_other2, grad3, grad4, to_other3 = meet(cfg, tiles, blocks, [to_other2], 3)

    back0 = send(to_other0, way["cores"])
    back1 = send(to_other1, way["cores"])
    back2 = send(to_other2, way["cores"])
    back3 = send(to_other3, way["cores"])

    def own(grad):
        return pick(leader, 0.0, grad)

    lead_grad = pick(x == 0, grad0, grad4) + grad1 + grad2 + grad3
    sum1 = own(grad1) + back1
    sum3 = own(grad3) + back3
    sum4 = own(grad4) + send(sum3, back(way["late"]))
    sum2 = own(grad2) + back2
    sum2 = sum2 + send(pick(inner, sum1, sum3), back(way["side"]))
    sum2 = sum2 + send(sum4, back(way["far"]))
    from_near = send(sum2, back(way["near"]))
    outgoing = pick(at(0, 0), sum2, pick(at(0, 1), lead_grad, sum1))
    from_first = send(outgoing, back(way["first"]))
    sum0 = own(grad0) + back0 + from_near + pick(at(1, 0), 0.0, from_first)
    head_grad = pick(c == 0, lead_grad, from_first)
    crossing = jnp.stack([sum0[1], pick(c == 0, head_grad[1], head_grad[0])])
    crossed = send(crossing, way["cores"])
    same = pick(origin, sum0[0] + crossed[0], sum0[0])
    head_half = pick(c == 0, head_grad[0], head_grad[1]) + crossed[1]
    upper = pick(origin, head_half, pick(c == 0, same, crossed[0]))
    lower = pick(origin, same, pick(c == 0, crossed[0], same))
    total = send(jnp.stack([upper, lower]), way["gather"])[None]
    new_state = state + total * total
    step = total / jnp.sqrt(new_state)
    return (step, new_state)


def solution(mesh):
    in_specs = (
        P("blk", None, "rep", None),
        P("blk", None, "rep", None),
        P("blk", None, None, None),
    )
    out_specs = (P("blk", None, "rep", None), P("blk", None, "rep", None))
    return jax.shard_map(body, mesh=mesh, in_specs=in_specs, out_specs=out_specs, check_vma=False)
```

```python
import functools
import jax
import jax.numpy as jnp
import numpy as np
from jax import lax
from jax.experimental import pallas as pl
from jax.experimental.pallas import tpu as pltpu
from jax.sharding import PartitionSpec as P

clip_bound = 2.0
AXES = ("blk", "rep")


def place(row, side, core, plane):
    return ((2 * row + side) * 2 + core) * 2 + plane


def routes(rows):
    own = [(r, s, c, x) for r in range(rows) for s in range(2) for c in range(2) for x in range(2)]
    gather = [(place(r, s, c, x), place(r, s, x, c)) for r, s, c, x in own]
    cores = [(place(r, s, c, x), place(r, s, 1 - c, x)) for r, s, c, x in own]
    near, far, side, late = [], [], [], []
    for r, s, c, x in own:
        me = place(r, s, c, x)
        if c == 0:
            to = place(r + 1, s, 0, x) if r < rows - 1 else place(r, 1 - s, 1, 1 - x)
            near.append((me, to))
            far.append((me, to))
        elif r > 0:
            to = place(r - 1, s, 1, x)
            near.append((me, to))
            far.append((me, to))
        elif x == 1:
            to = place(0, 1 - s, 0, 1)
            near.append((me, to))
            far.append((me, to))
        else:
            if s == 1:
                near.append((me, place(0, 1, 0, 0)))
                far.append((me, place(0, 1, 0, 0)))
        side.append((me, place(r, 1 - s, c, x)))
    first = [(place(r, s, c, x), place(r, 1 - s, c, x)) for r, s, c, x in own if c == s]
    first.append((place(0, 0, 1, 0), place(0, 0, 0, 1)))
    first.append((place(1, 0, 1, 0), place(0, 0, 0, 0)))
    late = [(place(r, s, c, x), place(r, 1 - s, c, x)) for r, s, c, x in own if c != s]
    return dict(gather=gather, cores=cores, near=near, far=far, side=side, first=first, late=late)


def inner_index(device):
    return (device // 2) % 2 == (device // 4) % 2


def send(block, pairs):
    return lax.ppermute(block, AXES, pairs)


def back(pairs):
    return [(b, a) for a, b in pairs]


def residual_of(scores, count_tile):
    amount = count_tile.astype(jnp.float32)
    present = count_tile > 0
    clamped = jnp.maximum(amount, 1.0)
    weight = 0.1 + 0.25 * jnp.sqrt(clamped)
    kept = weight * jnp.clip(scores - jnp.log(clamped), -clip_bound, clip_bound)
    return jnp.where(present, kept, 0.5 / (1.0 + jnp.exp(-scores)))


def split(value):
    high = value.astype(jnp.bfloat16)
    return high, (value - high.astype(jnp.float32)).astype(jnp.bfloat16)


def dot(left, right, dims):
    return lax.dot_general(left, right, (dims, ((), ())), preferred_element_type=jnp.float32)


ACTIVE, MAIN, OTHER, TILE, SWAP, CORE, OUT_MAIN, OUT_OTHER, ZERO = range(9)
FIRST_ROW = (0, 1, 2, 4)
BLOCKS = (
    ("head", "main0", "other0"),
    ("head", "first", "main2", "other0", "other_first", "other2"),
    ("head", "first", "side", "main2", "main4", "other0", "other_first", "other2", "other_side"),
    ("head", "first", "side", "late", "main4", "other2", "other_side", "other_late"),
)
OUTS = (
    ("g0", "o0"),
    ("o0", "g1", "g2", "o1", "o2"),
    ("o0", "g1", "g2", "o1", "o2", "g3", "g4", "o3"),
    ("o2", "g3", "g4", "o3"),
)


def plan(players):
    chips = players // 2
    table = np.zeros((players, 2, 5, 9), np.int32)
    for player in range(players):
        for x in range(2):
            chip, c = player // 2, player % 2
            native, inner = c == x, c == chip % 2
            main = {0: "main0", 1: "side" if inner else "first", 2: "main2", 3: "late" if inner else "side", 4: "main4"}
            other = {
                0: "other0",
                1: "other_first" if inner else "other_side",
                2: "other2",
                3: "other_side" if inner else "other_late",
            }
            if native:
                turns = [(0, 0), (1, 2), (2, 1), None, (3, 3)]
            elif inner:
                turns = [None, (1, 1), (2, 0), (2, 3), (3, 2)]
            else:
                turns = [None, (1, 0), (2, 1), (2, 2), (3, 3)]
            for line, turn in enumerate(turns):
                stage = (0, 1, 2, 2, 3)[line]
                row = table[player, x, line]
                row[:] = -1
                row[ACTIVE] = turn is not None
                row[CORE] = c
                if turn is not None:
                    k = turn[1]
                    ahead = k if native else k + 1
                    behind_up = ahead if c == 0 else k
                    ahead_low = ahead if c == 1 else k
                    turned_up = chip - behind_up < 0 and player > 0
                    turned_low = chip + ahead_low >= chips
                    source = main[ahead]
                    if player == 0:
                        source = "head" if x == 0 else "first"
                    row[MAIN] = BLOCKS[stage].index(source)
                    row[OTHER] = BLOCKS[stage].index(other[k])
                    row[TILE] = 2 * k + (0 if native else 1)
                    row[SWAP] = turned_up == turned_low
                    row[OUT_MAIN] = OUTS[stage].index("g%d" % ahead)
                    row[OUT_OTHER] = OUTS[stage].index("o%d" % k)
                elif line == 0:
                    row[ZERO] = OUTS[stage].index("g0")
                else:
                    row[ZERO] = OUTS[stage].index("g4")
    return table


def meet_kernel(lines, n_blocks, n_out, n_kept, cfg, counts, *refs):
    blocks = refs[:n_blocks]
    outs = refs[n_blocks + n_kept : n_blocks + n_kept + n_out]
    tile, raw, high, low, res_high, res_low, grad, sems, out_sems = refs[n_blocks + n_kept + n_out :]
    half = raw.shape[1] // 2
    size = tile.shape[0]
    pad = high.shape[2]
    if pad > half:
        rest = jnp.zeros((2, 2, pad - (half - half % 16), size), jnp.bfloat16)
        high[:, :, half - half % 16 : pad, :] = rest
        low[:, :, half - half % 16 : pad, :] = rest
    for q in lines:

        @pl.when(cfg[q, ACTIVE] == 1)
        def _():
            pltpu.make_async_copy(counts.at[cfg[q, TILE]], tile, sems.at[2]).start()
            for b in range(n_blocks):
                for which, column in ((0, MAIN), (1, OTHER)):

                    @pl.when(cfg[q, column] == b)
                    def _():
                        pltpu.make_async_copy(blocks[b], raw.at[which], sems.at[which]).start()

            core = cfg[q, CORE]
            for which in range(2):
                pltpu.make_async_copy(blocks[0], raw.at[which], sems.at[which]).wait()
                for h in range(2):
                    to = h if which == 0 else jnp.where(cfg[q, SWAP] == 1, 1 - h, h)
                    hi, lo = split(raw[which, h * half : (h + 1) * half, :])
                    high[which, to, 0:half, :] = hi
                    low[which, to, 0:half, :] = lo
            pltpu.make_async_copy(counts.at[0], tile, sems.at[2]).wait()
            up_h = high[core].reshape(2 * pad, size)
            up_l = low[core].reshape(2 * pad, size)
            lo_h = high[1 - core].reshape(2 * pad, size)
            lo_l = low[1 - core].reshape(2 * pad, size)
            right = jnp.concatenate([lo_h, lo_l, lo_h], axis=0)
            left = jnp.concatenate([up_h, up_h, up_l], axis=0)
            rows = min(size, 256)
            for s in range(size // rows):
                band = slice(s * rows, (s + 1) * rows)
                scores = dot(left[:, band], right, ((0,), (0,)))
                hi, lo = split(residual_of(scores, tile[band, :]))
                res_high[band, :] = hi
                res_low[band, :] = lo
            rh = res_high[...]
            rl = res_low[...]
            across = ((1,), (1,))
            along = ((1,), (0,))
            grad_upper = dot(lo_h, rh, across) + dot(lo_l, rh, across) + dot(lo_h, rl, across)
            grad_lower = dot(up_h, rh, along) + dot(up_l, rh, along) + dot(up_h, rl, along)
            for h in range(2):
                band = slice(h * pad, h * pad + half)
                for which, value in ((0, grad_upper), (1, grad_lower)):
                    target = jnp.where(core == 0, which, 1 - which)
                    to = jnp.where((cfg[q, SWAP] == 1) & (target == 1), 1 - h, h)
                    grad[target, pl.ds(pl.multiple_of(to * half, 8), half), :] = value[band, :]
            for o in range(n_out):
                for which, column in ((0, OUT_MAIN), (1, OUT_OTHER)):

                    @pl.when(cfg[q, column] == o)
                    def _():
                        pltpu.make_async_copy(grad.at[which], outs[o], out_sems.at[which]).start()

            for which in range(2):
                pltpu.make_async_copy(grad.at[which], outs[0], out_sems.at[which]).wait()

        @pl.when(cfg[q, ZERO] >= 0)
        def _():
            grad[0] = jnp.zeros(grad.shape[1:], jnp.float32)
            for o in range(n_out):

                @pl.when(cfg[q, ZERO] == o)
                def _():
                    copy = pltpu.make_async_copy(grad.at[0], outs[o], out_sems.at[0])
                    copy.start()
                    copy.wait()


def meet(stage, cfg, counts, blocks, slots):
    lines = range(FIRST_ROW[stage], (FIRST_ROW + (5,))[stage + 1])
    meetings = len(lines)
    blocks = [blocks[name] for name in BLOCKS[stage]]
    kept = [slots[name] for name in OUTS[stage] if name in slots]
    fresh = len(OUTS[stage]) - len(kept)
    double, size = blocks[0].shape
    half = double // 2
    pad = -(-half // 16) * 16
    n_out = len(kept) + fresh
    shape = jax.ShapeDtypeStruct(blocks[0].shape, jnp.float32)
    hbm = pl.BlockSpec(memory_space=pl.ANY)
    results = pl.pallas_call(
        functools.partial(meet_kernel, lines, len(blocks), n_out, len(kept)),
        out_shape=[shape] * n_out,
        in_specs=[pl.BlockSpec(memory_space=pltpu.SMEM)] + [hbm] * (1 + len(blocks) + len(kept)),
        out_specs=[hbm] * n_out,
        input_output_aliases={2 + len(blocks) + i: i for i in range(len(kept))},
        scratch_shapes=[
            pltpu.VMEM((size, size), jnp.int32),
            pltpu.VMEM((2, double, size), jnp.float32),
            pltpu.VMEM((2, 2, pad, size), jnp.bfloat16),
            pltpu.VMEM((2, 2, pad, size), jnp.bfloat16),
            pltpu.VMEM((size, size), jnp.bfloat16),
            pltpu.VMEM((size, size), jnp.bfloat16),
            pltpu.VMEM((2, double, size), jnp.float32),
            pltpu.SemaphoreType.DMA((3,)),
            pltpu.SemaphoreType.DMA((2,)),
        ],
        cost_estimate=pl.CostEstimate(
            flops=meetings * 18 * half * 2 * size * size,
            bytes_accessed=meetings * (4 * size * size + 32 * half * size),
            transcendentals=meetings * 3 * size * size,
        ),
    )(cfg, counts, *blocks, *kept)
    return dict(slots, **dict(zip(OUTS[stage], results)))


def body(factors, state, counts):
    players = lax.axis_size("blk")
    chips = players // 2
    way = routes(chips // 2)
    player = lax.axis_index("blk")
    x = lax.axis_index("rep")
    chip, c = player // 2, player % 2
    tiles = counts[0]

    def at(player_, plane):
        return (player == player_) & (x == plane)

    origin = (chip == 0) & (x == 0)

    def pick(cond, one, two):
        return jnp.where(cond, one, two)

    features, size = factors.shape[2:]
    half = -(-features // 8) * 8
    cfg = lax.dynamic_slice(jnp.asarray(plan(players)), (player, x, 0, 0), (1, 1, 5, 9))[0, 0]
    mine = send(factors[0], way["gather"])
    mine = jnp.pad(mine, ((0, 0), (0, half - features), (0, 0))).reshape(2 * half, size)
    theirs = send(mine, way["cores"])
    first_upper = pick(origin, 1, 0)
    main_at = pick(c == 0, first_upper, 1)
    other_at = pick(c == 0, 1, first_upper)

    def take(stack, i):
        return lax.dynamic_slice_in_dim(stack, i * half, half, 0)

    got = {}
    slots = {}
    got["main0"] = jnp.concatenate([take(mine, main_at), take(theirs, main_at)])
    got["other0"] = jnp.concatenate([take(theirs, other_at), take(mine, other_at)])
    got["head"] = pick(
        c == 0, jnp.concatenate([mine[:half], theirs[:half]]), jnp.concatenate([theirs[:half], mine[:half]])
    )

    def after(names, slots):
        held = [got[name] for name in names]
        held, slots = lax.optimization_barrier((held, slots))
        got.update(zip(names, held))
        return slots

    got["first"] = send(pick(at(1, 0), got["head"], got["main0"]), way["first"])
    got["near"] = send(got["main0"], way["near"])
    slots = meet(0, cfg, tiles, got, slots)
    slots = after(["first", "near"], slots)
    got["main2"] = pick(at(0, 0), got["first"], got["near"])
    got["other2"] = send(got["main2"], way["cores"])
    got["side"] = send(got["main2"], way["side"])
    got["main4"] = send(got["main2"], way["far"])
    got["other_first"] = send(got["first"], way["cores"])
    slots = meet(1, cfg, tiles, got, slots)
    slots = after(["side", "main4"], slots)
    got["late"] = send(got["main4"], way["late"])
    got["other_side"] = send(got["side"], way["cores"])
    slots = meet(2, cfg, tiles, got, slots)
    slots = after(["late"], slots)
    got["other_late"] = send(got["late"], way["cores"])

    leader = player == 0

    def own(grad):
        return pick(leader, 0.0, grad)

    sum0 = own(slots["g0"]) + send(slots["o0"], way["cores"])
    sum1 = own(slots["g1"]) + send(slots["o1"], way["cores"])
    back_side = back(way["side"])
    early = send(sum1, [pair for pair in back_side if inner_index(pair[0])])
    slots = meet(3, cfg, tiles, got, slots)
    (early,), slots = lax.optimization_barrier(([early], slots))
    sum3 = own(slots["g3"]) + send(slots["o3"], way["cores"])
    sum4 = own(slots["g4"]) + send(sum3, back(way["late"]))
    sum2 = own(slots["g2"]) + send(slots["o2"], way["cores"]) + early
    sum4, sum3 = lax.optimization_barrier((sum4, sum3))
    from_far = send(sum4, back(way["far"]))
    from_side = send(sum3, [pair for pair in back_side if not inner_index(pair[0])])
    sum2 = sum2 + from_side + from_far
    from_near = send(sum2, back(way["near"]))
    lead_grad = pick(x == 0, slots["g0"], slots["g4"]) + slots["g1"] + slots["g2"] + slots["g3"]
    outgoing = pick(at(0, 0), sum2, pick(at(0, 1), lead_grad, sum1))
    from_first = send(outgoing, back(way["first"]))
    sum0 = sum0 + from_near + pick(at(1, 0), 0.0, from_first)
    head_grad = pick(c == 0, lead_grad, from_first)
    crossing = jnp.concatenate([sum0[half:], pick(c == 0, head_grad[half:], head_grad[:half])])
    crossed = send(crossing, way["cores"])
    same = pick(origin, sum0[:half] + crossed[:half], sum0[:half])
    head_half = pick(c == 0, head_grad[:half], head_grad[half:]) + crossed[half:]
    upper = pick(origin, head_half, pick(c == 0, same, crossed[:half]))
    lower = pick(origin, same, pick(c == 0, crossed[:half], same))
    total = send(jnp.stack([upper[:features], lower[:features]]), way["gather"])[None]
    new_state = state + total * total
    step = total / jnp.sqrt(new_state)
    return (step, new_state)


def solution(mesh):
    in_specs = (
        P("blk", None, "rep", None),
        P("blk", None, "rep", None),
        P("blk", None, None, None),
    )
    out_specs = (P("blk", None, "rep", None), P("blk", None, "rep", None))
    return jax.shard_map(body, mesh=mesh, in_specs=in_specs, out_specs=out_specs, check_vma=False)
```

```python
import functools
import jax
import jax.numpy as jnp
import numpy as np
from jax import lax
from jax.experimental import pallas as pl
from jax.experimental.pallas import tpu as pltpu
from jax.sharding import PartitionSpec as P

clip_bound = 2.0
AXES = ("blk", "rep")


def place(row, side, core, plane):
    return ((2 * row + side) * 2 + core) * 2 + plane


def inner(side, core):
    return core == side


def routes(rows):
    every = [(r, s, c, x) for r in range(rows) for s in range(2) for c in range(2) for x in range(2)]
    way = {name: [] for name in ("keep", "upper", "lower", "cores", "first", "near", "side", "far", "late")}
    way.update({name: [] for name in ("home_one", "home_three", "home_tail")})
    for r, s, c, x in every:
        me = place(r, s, c, x)
        way["cores"].append((me, place(r, s, 1 - c, x)))
        if c == x:
            way["keep"].append((me, place(r, s, 1 - c, x)))
        else:
            way["upper"].append((me, place(r, s, 0, c)))
            way["lower"].append((me, place(r, s, 1, c)))
        beside = place(r, 1 - s, c, x)
        way["side"].append((me, beside))
        if inner(s, c):
            if (r, s, c, x) != (0, 0, 0, 0):
                way["first"].append((me, beside))
        else:
            way["late"].append((me, beside))
            way["home_three"].append((me, beside))
        if (r, s, c, x) != (0, 1, 0, 0):
            way["home_one"].append((me, beside))
        if c == 0 and r == rows - 1:
            to = place(r, 1 - s, 1, 1 - x)
        elif c == 0:
            to = place(r + 1, s, 0, x)
        elif r > 0:
            to = place(r - 1, s, 1, x)
        elif x == 1:
            to = place(0, 1 - s, 0, 1)
        elif s == 1:
            to = place(0, 1, 0, 0)
        else:
            continue
        way["far"].append((me, to))
        if (r, s, c, x) != (0, 0, 0, 0):
            way["near"].append((me, to))
    way["near"].append((place(0, 0, 1, 0), place(1, 0, 0, 0)))
    special = [
        (place(0, 0, 1, 0), place(0, 1, 0, 0)),
        (place(0, 0, 0, 0), place(0, 0, 0, 1)),
        (place(1, 0, 1, 0), place(0, 0, 0, 0)),
    ]
    way["first"] += special
    way["home_tail"] = back(special)
    for name in ("keep", "upper", "lower", "near", "far", "late"):
        way["home_" + name] = back(way[name])
    return way


def send(block, pairs):
    return lax.ppermute(block, AXES, pairs)


def back(pairs):
    return [(b, a) for a, b in pairs]


def count_terms(count_tile):
    clamped = jnp.maximum(count_tile.astype(jnp.float32), 1.0)
    weight = 0.1 + 0.25 * jnp.sqrt(clamped)
    return jnp.where(count_tile > 0, weight, 0.0), jnp.log(clamped)


def residual_of(scores, weight, log_count):
    kept = weight * jnp.clip(scores - log_count, -clip_bound, clip_bound)
    return jnp.where(weight > 0.0, kept, 0.25 + 0.25 * jnp.tanh(0.5 * scores))


def terms_kernel(first, counts, weight, log_count):
    weight[...], log_count[...] = count_terms(counts[...])


def prepare(counts, first):
    rounds, size, _ = counts.shape
    block = (1, size, size)
    shape = jax.ShapeDtypeStruct((rounds // 2, size, size), jnp.float32)
    return pl.pallas_call(
        terms_kernel,
        out_shape=[shape, shape],
        grid_spec=pltpu.PrefetchScalarGridSpec(
            num_scalar_prefetch=1,
            grid=(rounds // 2,),
            in_specs=[pl.BlockSpec(block, lambda k, first: (2 * k + first[0], 0, 0))],
            out_specs=[pl.BlockSpec(block, lambda k, first: (k, 0, 0))] * 2,
        ),
        compiler_params=pltpu.CompilerParams(vmem_limit_bytes=28 * size * size + (2 << 20)),
        cost_estimate=pl.CostEstimate(
            flops=40 * rounds // 2 * size * size, bytes_accessed=6 * rounds * size * size, transcendentals=rounds * size * size
        ),
    )(first, counts)


def split(value):
    high = value.astype(jnp.bfloat16)
    return high, (value - high.astype(jnp.float32)).astype(jnp.bfloat16)


def dot(left, right, dims):
    return lax.dot_general(left, right, (dims, ((), ())), preferred_element_type=jnp.float32)


ACTIVE, MAIN, OTHER, TILE, SWAP, CORE, OUT_MAIN, OUT_OTHER, ZERO = range(9)
FIRST_ROW = (0, 1, 2, 4)
BLOCKS = (
    ("main0", "other0"),
    ("main0", "first", "main2", "other0", "other_first", "other2"),
    ("main0", "first", "side", "main2", "main4", "other0", "other_first", "other2", "other_side"),
    ("main0", "first", "side", "late", "main4", "other2", "other_side", "other_late"),
)
OUTS = (
    ("g0", "o0"),
    ("g0", "o0", "g1", "g2", "o1", "o2"),
    ("o0", "g1", "g2", "o1", "o2", "g3", "g4", "o3"),
    ("o2", "g3", "g4", "o3"),
)


def plan(players):
    chips = players // 2
    table = np.zeros((players, 2, 5, 9), np.int32)
    for player in range(players):
        for x in range(2):
            chip, c = player // 2, player % 2
            native, within = c == x, inner(chip % 2, c)
            main = {0: "main0", 1: "side" if within else "first", 2: "main2", 3: "late" if within else "side", 4: "main4"}
            other = {
                0: "other0",
                1: "other_first" if within else "other_side",
                2: "other2",
                3: "other_side" if within else "other_late",
            }
            if native:
                turns = [(0, 0), (1, 2), (2, 1), None, (3, 3)]
            elif within:
                turns = [None, (1, 1), (2, 0), (2, 3), (3, 2)]
            else:
                turns = [None, (1, 0), (2, 1), (2, 2), (3, 3)]
            for line, turn in enumerate(turns):
                stage = (0, 1, 2, 2, 3)[line]
                row = table[player, x, line]
                row[:] = -1
                row[ACTIVE] = turn is not None
                row[CORE] = c
                if turn is not None:
                    k = turn[1]
                    ahead = k if native else k + 1
                    ahead_low = ahead if c == 1 else k
                    turned = chip + ahead_low >= chips
                    source, partner, out = main[ahead], other[k], "o%d" % k
                    if player == 0:
                        source = "main0" if x == 0 else "first"
                        turned = x == 1
                    if player == 1 and x == 0 and k == 0:
                        partner, out = "main0", "g0"
                    row[MAIN] = BLOCKS[stage].index(source)
                    row[OTHER] = BLOCKS[stage].index(partner)
                    row[TILE] = k
                    row[SWAP] = turned
                    row[OUT_MAIN] = OUTS[stage].index("g%d" % ahead)
                    row[OUT_OTHER] = OUTS[stage].index(out)
                elif line == 0:
                    row[ZERO] = OUTS[stage].index("o0" if player == 1 and x == 0 else "g0")
                else:
                    row[ZERO] = OUTS[stage].index("g4")
    return table


def meet_kernel(lines, n_blocks, n_out, n_kept, cfg, weights, logs, *refs):
    blocks = refs[:n_blocks]
    outs = refs[n_blocks + n_kept : n_blocks + n_kept + n_out]
    weight, log_count, raw, high, low, res_high, res_low, grad, sems, out_sems = refs[n_blocks + n_kept + n_out :]
    half = raw.shape[1] // 2
    size = weight.shape[0]
    pad = high.shape[2]
    if pad > half:
        rest = jnp.zeros((2, 2, pad - (half - half % 16), size), jnp.bfloat16)
        high[:, :, half - half % 16 : pad, :] = rest
        low[:, :, half - half % 16 : pad, :] = rest
    for q in lines:

        @pl.when(cfg[q, ACTIVE] == 1)
        def _():
            for b in range(n_blocks):
                for which, column in ((0, MAIN), (1, OTHER)):

                    @pl.when(cfg[q, column] == b)
                    def _():
                        pltpu.make_async_copy(blocks[b], raw.at[which], sems.at[which]).start()

            pltpu.make_async_copy(weights.at[cfg[q, TILE]], weight, sems.at[2]).start()
            pltpu.make_async_copy(logs.at[cfg[q, TILE]], log_count, sems.at[3]).start()
            core = cfg[q, CORE]
            for which in range(2):
                pltpu.make_async_copy(blocks[0], raw.at[which], sems.at[which]).wait()
                for h in range(2):
                    to = h if which == 0 else jnp.where(cfg[q, SWAP] == 1, 1 - h, h)
                    hi, lo = split(raw[which, h * half : (h + 1) * half, :])
                    high[which, to, 0:half, :] = hi
                    low[which, to, 0:half, :] = lo
            pltpu.make_async_copy(weights.at[0], weight, sems.at[2]).wait()
            pltpu.make_async_copy(logs.at[0], log_count, sems.at[3]).wait()
            up_h = high[core].reshape(2 * pad, size)
            up_l = low[core].reshape(2 * pad, size)
            lo_h = high[1 - core].reshape(2 * pad, size)
            lo_l = low[1 - core].reshape(2 * pad, size)
            right = jnp.concatenate([lo_h, lo_l, lo_h], axis=0)
            left = jnp.concatenate([up_h, up_h, up_l], axis=0)
            rows = min(size, 256)
            for s in range(size // rows):
                band = slice(s * rows, (s + 1) * rows)
                scores = dot(left[:, band], right, ((0,), (0,)))
                hi, lo = split(residual_of(scores, weight[band, :], log_count[band, :]))
                res_high[band, :] = hi
                res_low[band, :] = lo
            rh = res_high[...]
            rl = res_low[...]
            across = ((1,), (1,))
            along = ((1,), (0,))
            grad_upper = dot(lo_h, rh, across) + dot(lo_l, rh, across) + dot(lo_h, rl, across)
            grad_lower = dot(up_h, rh, along) + dot(up_l, rh, along) + dot(up_h, rl, along)
            for h in range(2):
                band = slice(h * pad, h * pad + half)
                for which, value in ((0, grad_upper), (1, grad_lower)):
                    target = jnp.where(core == 0, which, 1 - which)
                    to = jnp.where((cfg[q, SWAP] == 1) & (target == 1), 1 - h, h)
                    grad[target, pl.ds(pl.multiple_of(to * half, 8), half), :] = value[band, :]
            for o in range(n_out):
                for which, column in ((0, OUT_MAIN), (1, OUT_OTHER)):

                    @pl.when(cfg[q, column] == o)
                    def _():
                        pltpu.make_async_copy(grad.at[which], outs[o], out_sems.at[which]).start()

            for which in range(2):
                pltpu.make_async_copy(grad.at[which], outs[0], out_sems.at[which]).wait()

        @pl.when(cfg[q, ZERO] >= 0)
        def _():
            grad[0] = jnp.zeros(grad.shape[1:], jnp.float32)
            for o in range(n_out):

                @pl.when(cfg[q, ZERO] == o)
                def _():
                    copy = pltpu.make_async_copy(grad.at[0], outs[o], out_sems.at[0])
                    copy.start()
                    copy.wait()


def vmem_budget(double, size):
    return 40 * double * size + 24 * size * size + (2 << 20)


def meet(stage, cfg, terms, blocks, slots):
    lines = range(FIRST_ROW[stage], (FIRST_ROW + (5,))[stage + 1])
    meetings = len(lines)
    blocks = [blocks[name] for name in BLOCKS[stage]]
    kept = [slots[name] for name in OUTS[stage] if name in slots]
    fresh = len(OUTS[stage]) - len(kept)
    double, size = blocks[0].shape
    half = double // 2
    pad = -(-half // 16) * 16
    n_out = len(kept) + fresh
    shape = jax.ShapeDtypeStruct(blocks[0].shape, jnp.float32)
    hbm = pl.BlockSpec(memory_space=pl.ANY)
    results = pl.pallas_call(
        functools.partial(meet_kernel, lines, len(blocks), n_out, len(kept)),
        out_shape=[shape] * n_out,
        in_specs=[pl.BlockSpec(memory_space=pltpu.SMEM)] + [hbm] * (2 + len(blocks) + len(kept)),
        out_specs=[hbm] * n_out,
        input_output_aliases={3 + len(blocks) + i: i for i in range(len(kept))},
        scratch_shapes=[
            pltpu.VMEM((size, size), jnp.float32),
            pltpu.VMEM((size, size), jnp.float32),
            pltpu.VMEM((2, double, size), jnp.float32),
            pltpu.VMEM((2, 2, pad, size), jnp.bfloat16),
            pltpu.VMEM((2, 2, pad, size), jnp.bfloat16),
            pltpu.VMEM((size, size), jnp.bfloat16),
            pltpu.VMEM((size, size), jnp.bfloat16),
            pltpu.VMEM((2, double, size), jnp.float32),
            pltpu.SemaphoreType.DMA((4,)),
            pltpu.SemaphoreType.DMA((2,)),
        ],
        compiler_params=pltpu.CompilerParams(vmem_limit_bytes=vmem_budget(double, size)),
        cost_estimate=pl.CostEstimate(
            flops=meetings * 18 * half * 2 * size * size,
            bytes_accessed=meetings * (4 * size * size + 32 * half * size),
            transcendentals=meetings * 3 * size * size,
        ),
    )(cfg, *terms, *blocks, *kept)
    return dict(slots, **dict(zip(OUTS[stage], results)))


def body(factors, state, counts):
    players = lax.axis_size("blk")
    chips = players // 2
    way = routes(chips // 2)
    player = lax.axis_index("blk")
    x = lax.axis_index("rep")
    chip, c = player // 2, player % 2
    origin = (player == 0) & (x == 0)
    within = c == chip % 2
    leader = player == 0
    pick = jnp.where

    features, size = factors.shape[2:]
    half = -(-features // 8) * 8
    rest = ((0, half - features), (0, 0))
    upper, lower = jnp.pad(factors[0, 0], rest), jnp.pad(factors[0, 1], rest)
    kept = send(pick(c == 0, lower, upper), way["keep"])
    far_upper = send(upper, way["upper"])
    far_lower = send(lower, way["lower"])
    cfg = lax.dynamic_slice(jnp.asarray(plan(players)), (player, x, 0, 0), (1, 1, 5, 9))[0, 0]
    terms = prepare(counts[0], pick(c == x, 0, 1)[None])
    (kept, far_upper, far_lower), cfg, terms = lax.optimization_barrier(((kept, far_upper, far_lower), cfg, terms))
    got = {}
    slots = {}
    got["main0"] = jnp.concatenate(
        [pick(c == x, pick(c == 0, upper, lower), kept), pick(c == 0, far_upper, far_lower)]
    )

    def after(names, slots):
        held = [got[name] for name in names]
        held, slots = lax.optimization_barrier((held, slots))
        got.update(zip(names, held))
        return slots

    got["first"] = send(got["main0"], way["first"])
    got["near"] = send(got["main0"], way["near"])
    got["other0"] = send(got["main0"], way["cores"])
    slots = meet(0, cfg, terms, got, slots)
    slots = after(["first", "near"], slots)
    got["main2"] = pick(origin, got["first"], got["near"])
    got["other2"] = send(got["main2"], way["cores"])
    got["side"] = send(got["main2"], way["side"])
    got["main4"] = send(got["main2"], way["far"])
    got["other_first"] = send(got["first"], way["cores"])
    slots = meet(1, cfg, terms, got, slots)
    slots = after(["side", "main4"], slots)
    got["late"] = send(got["main4"], way["late"])
    got["other_side"] = send(got["side"], way["cores"])
    slots = meet(2, cfg, terms, got, slots)
    slots = after(["late"], slots)
    got["other_late"] = send(got["late"], way["cores"])

    def own(grad):
        return pick(leader, 0.0, grad)

    near0 = send(slots["o0"], way["cores"])
    sum1 = own(slots["g1"]) + send(slots["o1"], way["cores"])
    one = send(sum1, way["home_one"])
    slots = meet(3, cfg, terms, got, slots)
    (one,), slots = lax.optimization_barrier(([one], slots))
    sum3 = own(slots["g3"]) + send(slots["o3"], way["cores"])
    sum4 = own(slots["g4"]) + send(sum3, way["home_late"])
    sum4, sum3 = lax.optimization_barrier((sum4, sum3))
    from_far = send(sum4, way["home_far"])
    three = send(sum3, way["home_three"])
    lead = pick(x == 0, slots["g0"], slots["g4"]) + slots["g1"] + slots["g2"] + slots["g3"]
    sum2 = own(slots["g2"]) + send(slots["o2"], way["cores"]) + pick(within, 0.0, one) + three + from_far
    from_near = send(sum2, way["home_near"])
    tail = send(pick(origin, sum2, pick(leader, lead, sum1)), way["home_tail"])
    mine = pick(leader, pick(x == 0, lead, 0.0), slots["g0"])
    sum0 = mine + near0 + pick(within, one, 0.0) + from_near + tail
    here, there = sum0[:half], sum0[half:]
    kept = send(here, way["home_keep"])
    far_upper = send(there, way["home_upper"])
    far_lower = send(there, way["home_lower"])
    upper = pick(c == x, pick(c == 0, here, kept), far_upper)
    lower = pick(c == x, pick(c == 0, kept, here), far_lower)
    total = jnp.stack([upper[:features], lower[:features]])[None]
    new_state = state + total * total
    step = total / jnp.sqrt(new_state)
    return (step, new_state)


def solution(mesh):
    in_specs = (
        P("blk", None, "rep", None),
        P("blk", None, "rep", None),
        P("blk", None, None, None),
    )
    out_specs = (P("blk", None, "rep", None), P("blk", None, "rep", None))
    return jax.shard_map(body, mesh=mesh, in_specs=in_specs, out_specs=out_specs, check_vma=False)
```

```python
import functools
import jax
import jax.numpy as jnp
import numpy as np
from jax import lax
from jax.experimental import pallas as pl
from jax.experimental.pallas import tpu as pltpu
from jax.sharding import PartitionSpec as P


clip_bound = 2.0
AXES = ("blk", "rep")


def place(row, side, core, plane):
    return ((2 * row + side) * 2 + core) * 2 + plane


def inner(side, core):
    return core == side


def routes(rows):
    every = [(r, s, c, x) for r in range(rows) for s in range(2) for c in range(2) for x in range(2)]
    way = {name: [] for name in ("keep", "upper", "lower", "cores", "first", "near", "side", "far", "late")}
    way.update({name: [] for name in ("home_one", "home_three")})
    for r, s, c, x in every:
        me = place(r, s, c, x)
        way["cores"].append((me, place(r, s, 1 - c, x)))
        if c == x:
            way["keep"].append((me, place(r, s, 1 - c, x)))
        else:
            way["upper"].append((me, place(r, s, 0, c)))
            way["lower"].append((me, place(r, s, 1, c)))
        beside = place(r, 1 - s, c, x)
        way["side"].append((me, beside))
        if inner(s, c):
            way["home_one"].append((me, beside))
            if (r, s, c, x) != (0, 0, 0, 0):
                way["first"].append((me, beside))
        else:
            way["late"].append((me, beside))
            way["home_three"].append((me, beside))
        if c == 0 and r == rows - 1:
            to = place(r, 1 - s, 1, 1 - x)
        elif c == 0:
            to = place(r + 1, s, 0, x)
        elif r > 0:
            to = place(r - 1, s, 1, x)
        elif x == 1:
            to = place(0, 1 - s, 0, 1)
        elif s == 1:
            to = place(0, 1, 0, 0)
        else:
            continue
        way["far"].append((me, to))
        if (r, s, c, x) != (0, 0, 0, 0):
            way["near"].append((me, to))
    way["near"].append((place(0, 0, 1, 0), place(1, 0, 0, 0)))
    way["first"] += [
        (place(0, 0, 1, 0), place(0, 1, 0, 0)),
        (place(0, 0, 0, 0), place(0, 0, 0, 1)),
        (place(1, 0, 1, 0), place(0, 0, 0, 0)),
    ]
    for name in ("keep", "upper", "lower", "first", "near", "far", "late"):
        way["home_" + name] = back(way[name])
    return way


def send(block, pairs):
    return lax.ppermute(block, AXES, pairs)


def back(pairs):
    return [(b, a) for a, b in pairs]


def count_terms(count_tile):
    clamped = jnp.maximum(count_tile.astype(jnp.float32), 1.0)
    weight = 0.1 + 0.25 * jnp.sqrt(clamped)
    return jnp.where(count_tile > 0, weight, 0.0), jnp.log(clamped)


def residual_of(scores, weight, log_count):
    kept = weight * jnp.clip(scores - log_count, -clip_bound, clip_bound)
    return jnp.where(weight > 0.0, kept, 0.25 + 0.25 * jnp.tanh(0.5 * scores))


def terms_kernel(first, counts, weight, log_count, token):
    weight[...], log_count[...] = count_terms(counts[...])
    token[...] = jnp.zeros_like(token)


def prepare(counts, first):
    rounds, size, _ = counts.shape
    block = (1, size, size)
    shape = jax.ShapeDtypeStruct((rounds // 2, size, size), jnp.float32)
    return pl.pallas_call(
        terms_kernel,
        out_shape=[shape, shape, jax.ShapeDtypeStruct((8, 128), jnp.int32)],
        grid_spec=pltpu.PrefetchScalarGridSpec(
            num_scalar_prefetch=1,
            grid=(rounds // 2,),
            in_specs=[pl.BlockSpec(block, lambda k, first: (2 * k + first[0], 0, 0))],
            out_specs=[pl.BlockSpec(block, lambda k, first: (k, 0, 0))] * 2
            + [pl.BlockSpec((8, 128), lambda k, first: (0, 0))],
        ),
        compiler_params=pltpu.CompilerParams(vmem_limit_bytes=28 * size * size + (2 << 20)),
        cost_estimate=pl.CostEstimate(
            flops=40 * rounds // 2 * size * size, bytes_accessed=6 * rounds * size * size, transcendentals=rounds * size * size
        ),
    )(first, counts)


def split(value):
    high = value.astype(jnp.bfloat16)
    return high, (value - high.astype(jnp.float32)).astype(jnp.bfloat16)


def dot(left, right, dims):
    return lax.dot_general(left, right, (dims, ((), ())), preferred_element_type=jnp.float32)


ACTIVE, MAIN, OTHER, TILE, SWAP, CORE, OUT_MAIN, OUT_OTHER, ZERO = range(9)
FIRST_ROW = (0, 1, 2, 4)
BLOCKS = (
    ("main0", "other0"),
    ("main0", "first", "main2", "other0", "other_first", "other2"),
    ("main0", "first", "side", "main2", "main4", "other0", "other_first", "other2", "other_side"),
    ("main0", "first", "side", "late", "main4", "other2", "other_side", "other_late"),
)
OUTS = (
    ("g0", "o0"),
    ("g0", "o0", "g1", "g2", "o1", "o2"),
    ("o0", "g1", "g2", "o1", "o2", "g3", "g4", "o3"),
    ("o2", "g3", "g4", "o3"),
)


def plan(players):
    chips = players // 2
    table = np.zeros((players, 2, 5, 9), np.int32)
    for player in range(players):
        for x in range(2):
            chip, c = player // 2, player % 2
            native, within = c == x, inner(chip % 2, c)
            main = {0: "main0", 1: "side" if within else "first", 2: "main2", 3: "late" if within else "side", 4: "main4"}
            other = {
                0: "other0",
                1: "other_first" if within else "other_side",
                2: "other2",
                3: "other_side" if within else "other_late",
            }
            if native:
                turns = [(0, 0), (1, 2), (2, 1), None, (3, 3)]
            elif within:
                turns = [None, (1, 1), (2, 0), (2, 3), (3, 2)]
            else:
                turns = [None, (1, 0), (2, 1), (2, 2), (3, 3)]
            for line, turn in enumerate(turns):
                stage = (0, 1, 2, 2, 3)[line]
                row = table[player, x, line]
                row[:] = -1
                row[ACTIVE] = turn is not None
                row[CORE] = c
                if turn is not None:
                    k = turn[1]
                    ahead = k if native else k + 1
                    ahead_low = ahead if c == 1 else k
                    turned = chip + ahead_low >= chips
                    source, partner, out = main[ahead], other[k], "o%d" % k
                    if player == 0:
                        source = "main0" if x == 0 else "first"
                        turned = x == 1
                    if player == 1 and x == 0 and k == 0:
                        partner, out = "main0", "g0"
                    row[MAIN] = BLOCKS[stage].index(source)
                    row[OTHER] = BLOCKS[stage].index(partner)
                    row[TILE] = k
                    row[SWAP] = turned
                    row[OUT_MAIN] = OUTS[stage].index("g%d" % ahead)
                    row[OUT_OTHER] = OUTS[stage].index(out)
                elif line == 0:
                    row[ZERO] = OUTS[stage].index("o0" if player == 1 and x == 0 else "g0")
                else:
                    row[ZERO] = OUTS[stage].index("g4")
    return table


def meet_kernel(lines, n_blocks, n_out, n_kept, cfg, weights, logs, *refs):
    blocks = refs[:n_blocks]
    outs = refs[n_blocks + n_kept : n_blocks + n_kept + n_out]
    weight, log_count, raw, high, low, res_high, res_low, grad, sems, out_sems, term_sems = refs[n_blocks + n_kept + n_out :]
    half = raw.shape[1] // 2
    size = weight.shape[1]
    pad = high.shape[2]
    if pad > half:
        rest = jnp.zeros((2, 2, pad - (half - half % 16), size), jnp.bfloat16)
        high[:, :, half - half % 16 : pad, :] = rest
        low[:, :, half - half % 16 : pad, :] = rest

    def terms_copies(i, tile):
        return (
            pltpu.make_async_copy(weights.at[tile], weight.at[i], term_sems.at[0, i]),
            pltpu.make_async_copy(logs.at[tile], log_count.at[i], term_sems.at[1, i]),
        )

    for i, q in enumerate(lines):

        @pl.when(cfg[q, ACTIVE] == 1)
        def _():
            for copy in terms_copies(i, cfg[q, TILE]):
                copy.start()

    for i, q in enumerate(lines):

        @pl.when(cfg[q, ACTIVE] == 1)
        def _():
            for b in range(n_blocks):
                for which, column in ((0, MAIN), (1, OTHER)):

                    @pl.when(cfg[q, column] == b)
                    def _():
                        pltpu.make_async_copy(blocks[b], raw.at[which], sems.at[which]).start()

            core = cfg[q, CORE]
            for which in range(2):
                pltpu.make_async_copy(blocks[0], raw.at[which], sems.at[which]).wait()
                for h in range(2):
                    to = h if which == 0 else jnp.where(cfg[q, SWAP] == 1, 1 - h, h)
                    hi, lo = split(raw[which, h * half : (h + 1) * half, :])
                    high[which, to, 0:half, :] = hi
                    low[which, to, 0:half, :] = lo
            for copy in terms_copies(i, cfg[q, TILE]):
                copy.wait()
            up_h = high[core].reshape(2 * pad, size)
            up_l = low[core].reshape(2 * pad, size)
            lo_h = high[1 - core].reshape(2 * pad, size)
            lo_l = low[1 - core].reshape(2 * pad, size)
            right = jnp.concatenate([lo_h, lo_l, lo_h], axis=0)
            left = jnp.concatenate([up_h, up_h, up_l], axis=0)
            rows = min(size, 256)
            for s in range(size // rows):
                band = slice(s * rows, (s + 1) * rows)
                scores = dot(left[:, band], right, ((0,), (0,)))
                hi, lo = split(residual_of(scores, weight[i, band, :], log_count[i, band, :]))
                res_high[band, :] = hi
                res_low[band, :] = lo
            rh = res_high[...]
            rl = res_low[...]
            across = ((1,), (1,))
            along = ((1,), (0,))
            grad_upper = dot(lo_h, rh, across) + dot(lo_l, rh, across) + dot(lo_h, rl, across)
            grad_lower = dot(up_h, rh, along) + dot(up_l, rh, along) + dot(up_h, rl, along)
            for h in range(2):
                band = slice(h * pad, h * pad + half)
                for which, value in ((0, grad_upper), (1, grad_lower)):
                    target = jnp.where(core == 0, which, 1 - which)
                    to = jnp.where((cfg[q, SWAP] == 1) & (target == 1), 1 - h, h)
                    grad[target, pl.ds(pl.multiple_of(to * half, 8), half), :] = value[band, :]
            for o in range(n_out):
                for which, column in ((0, OUT_MAIN), (1, OUT_OTHER)):

                    @pl.when(cfg[q, column] == o)
                    def _():
                        pltpu.make_async_copy(grad.at[which], outs[o], out_sems.at[which]).start()

            for which in range(2):
                pltpu.make_async_copy(grad.at[which], outs[0], out_sems.at[which]).wait()

        @pl.when(cfg[q, ZERO] >= 0)
        def _():
            grad[0] = jnp.zeros(grad.shape[1:], jnp.float32)
            for o in range(n_out):

                @pl.when(cfg[q, ZERO] == o)
                def _():
                    copy = pltpu.make_async_copy(grad.at[0], outs[o], out_sems.at[0])
                    copy.start()
                    copy.wait()


def vmem_budget(double, size):
    return 40 * double * size + 32 * size * size + (2 << 20)


def meet(stage, cfg, terms, blocks, slots):
    lines = range(FIRST_ROW[stage], (FIRST_ROW + (5,))[stage + 1])
    meetings = len(lines)
    blocks = [blocks[name] for name in BLOCKS[stage]]
    kept = [slots[name] for name in OUTS[stage] if name in slots]
    fresh = len(OUTS[stage]) - len(kept)
    double, size = blocks[0].shape
    half = double // 2
    pad = -(-half // 16) * 16
    n_out = len(kept) + fresh
    shape = jax.ShapeDtypeStruct(blocks[0].shape, jnp.float32)
    hbm = pl.BlockSpec(memory_space=pl.ANY)
    results = pl.pallas_call(
        functools.partial(meet_kernel, lines, len(blocks), n_out, len(kept)),
        out_shape=[shape] * n_out,
        in_specs=[pl.BlockSpec(memory_space=pltpu.SMEM)] + [pl.BlockSpec(memory_space=pltpu.HBM)] * 2 + [hbm] * (len(blocks) + len(kept)),
        out_specs=[hbm] * n_out,
        input_output_aliases={3 + len(blocks) + i: i for i in range(len(kept))},
        scratch_shapes=[
            pltpu.VMEM((meetings, size, size), jnp.float32),
            pltpu.VMEM((meetings, size, size), jnp.float32),
            pltpu.VMEM((2, double, size), jnp.float32),
            pltpu.VMEM((2, 2, pad, size), jnp.bfloat16),
            pltpu.VMEM((2, 2, pad, size), jnp.bfloat16),
            pltpu.VMEM((size, size), jnp.bfloat16),
            pltpu.VMEM((size, size), jnp.bfloat16),
            pltpu.VMEM((2, double, size), jnp.float32),
            pltpu.SemaphoreType.DMA((2,)),
            pltpu.SemaphoreType.DMA((2,)),
            pltpu.SemaphoreType.DMA((2, meetings)),
        ],
        compiler_params=pltpu.CompilerParams(vmem_limit_bytes=vmem_budget(double, size)),
        cost_estimate=pl.CostEstimate(
            flops=meetings * 18 * half * 2 * size * size,
            bytes_accessed=meetings * (4 * size * size + 32 * half * size),
            transcendentals=meetings * 3 * size * size,
        ),
    )(cfg, *terms, *blocks, *kept)
    return dict(slots, **dict(zip(OUTS[stage], results)))


def play(factors, state, counts):
    players = lax.axis_size("blk")
    chips = players // 2
    way = routes(chips // 2)
    player = lax.axis_index("blk")
    x = lax.axis_index("rep")
    c = player % 2
    origin = (player == 0) & (x == 0)
    leader = player == 0
    pick = jnp.where

    features, _ = factors.shape[2:]
    half = -(-features // 8) * 8
    rest = ((0, half - features), (0, 0))
    upper, lower = jnp.pad(factors[0, 0], rest), jnp.pad(factors[0, 1], rest)
    kept = send(pick(c == 0, lower, upper), way["keep"])
    far_upper = send(upper, way["upper"])
    far_lower = send(lower, way["lower"])
    cfg = lax.dynamic_slice(jnp.asarray(plan(players)), (player, x, 0, 0), (1, 1, 5, 9))[0, 0]
    weights, logs, token = prepare(pltpu.with_memory_space_constraint(counts[0], pltpu.HBM), pick(c == x, 0, 1)[None])
    kept, far_upper, far_lower, token = lax.optimization_barrier((kept, far_upper, far_lower, token))
    cfg = cfg + token[0, 0]
    terms = [pltpu.with_memory_space_constraint(term, pltpu.HBM) for term in (weights, logs)]
    got = {}
    slots = {}
    got["main0"] = jnp.concatenate(
        [pick(c == x, pick(c == 0, upper, lower), kept), pick(c == 0, far_upper, far_lower)]
    )

    def after(names, slots):
        held = [got[name] for name in names]
        held, slots = lax.optimization_barrier((held, slots))
        got.update(zip(names, held))
        return slots

    got["first"] = send(got["main0"], way["first"])
    got["near"] = send(got["main0"], way["near"])
    got["other0"] = send(got["main0"], way["cores"])
    slots = meet(0, cfg, terms, got, slots)
    slots = after(["first", "near"], slots)
    got["main2"] = pick(origin, got["first"], got["near"])
    got["other2"] = send(got["main2"], way["cores"])
    got["side"] = send(got["main2"], way["side"])
    got["main4"] = send(got["main2"], way["far"])
    got["other_first"] = send(got["first"], way["cores"])
    slots = meet(1, cfg, terms, got, slots)
    slots = after(["side", "main4"], slots)
    got["late"] = send(got["main4"], way["late"])
    got["other_side"] = send(got["side"], way["cores"])
    slots = meet(2, cfg, terms, got, slots)
    slots = after(["late"], slots)
    got["other_late"] = send(got["late"], way["cores"])

    def own(grad):
        return pick(leader, 0.0, grad)

    near0 = send(slots["o0"], way["cores"])
    sum1 = own(slots["g1"]) + send(slots["o1"], way["cores"])
    one = send(sum1, way["home_one"])
    got["other_late"], sum1 = lax.optimization_barrier((got["other_late"], sum1))
    slots = meet(3, cfg, terms, got, slots)
    sum3 = own(slots["g3"]) + send(slots["o3"], way["cores"])
    sum3, one = lax.optimization_barrier((sum3, one))
    sum4 = own(slots["g4"]) + send(sum3, way["home_late"])
    sum4, sum3 = lax.optimization_barrier((sum4, sum3))
    from_far = send(sum4, way["home_far"])
    three = send(sum3, way["home_three"])
    lead = pick(x == 0, slots["g0"], slots["g4"]) + slots["g1"] + slots["g2"] + slots["g3"]
    sum2 = own(slots["g2"]) + send(slots["o2"], way["cores"]) + one + three + from_far
    from_near = send(sum2, way["home_near"])
    from_first = send(pick(origin, sum2, pick(leader, lead, sum1)), way["home_first"])
    mine = pick(leader, pick(x == 0, lead, 0.0), slots["g0"])
    sum0 = mine + near0 + from_near + from_first
    here, there = sum0[:half], sum0[half:]
    kept = send(here, way["home_keep"])
    far_upper = send(there, way["home_upper"])
    far_lower = send(there, way["home_lower"])
    upper = pick(c == x, pick(c == 0, here, kept), far_upper)
    lower = pick(c == x, pick(c == 0, kept, here), far_lower)
    total = jnp.stack([upper[:features], lower[:features]], axis=1)
    new_state = state[0].transpose(1, 0, 2) + total * total
    step = total / jnp.sqrt(new_state)
    return (step.transpose(1, 0, 2)[None], new_state.transpose(1, 0, 2)[None])


def solution(mesh):
    in_specs = (
        P("blk", None, "rep", None),
        P("blk", None, "rep", None),
        P("blk", None, None, None),
    )
    out_specs = (P("blk", None, "rep", None), P("blk", None, "rep", None))
    return jax.shard_map(play, mesh=mesh, in_specs=in_specs, out_specs=out_specs, check_vma=False)
```

```python
import functools
import jax
import jax.numpy as jnp
import numpy as np
from jax import lax
from jax.experimental import pallas as pl
from jax.experimental.pallas import tpu as pltpu
from jax.sharding import PartitionSpec as P


clip_bound = 2.0
AXES = ("blk", "rep")

MOVES = range(12)
KEEP, UPPER, LOWER, CORES, FIRST, NEAR, INTO, OUT, FAR, BEND, LATE, TURN = MOVES
TAIL = 12
HOME, OTHER = 100, 200
CROSS = 10


def place(row, side, core, plane):
    return ((2 * row + side) * 2 + core) * 2 + plane


def inner(side, core):
    return core == side


def turns_at(rows, row, core, plane):
    return row == rows - 1 and core == 1 or row == 0 and core == 0 and plane == 1


def spun(rows):
    pairs = [((0, 1, 1, 1), (0, 1, 0, 1)), ((0, 0, 1, 1), (1, 0, 0, 1))]
    pairs += [((1, 1, 1, 0), (0, 0, 0, 0)), ((1, 0, 1, 0), (0, 1, 0, 0))]
    for x in range(2):
        pairs.append(((rows - 1, 0, 0, 1 - x), (rows - 1, 0, 1, x)))
        pairs.append(((rows - 1, 1, 0, 1 - x), (rows - 2, 1, 1, x)))
    return pairs


def routes(rows):
    every = [(r, s, c, x) for r in range(rows) for s in range(2) for c in range(2) for x in range(2)]
    way = {move: [] for move in (*MOVES, OTHER + TURN)}
    origin = (0, 0, 0, 0)

    def add(move, source, target):
        way[move].append((place(*source), place(*target)))

    for me in every:
        r, s, c, x = me
        add(CORES, me, (r, s, 1 - c, x))
        if c == x:
            add(KEEP, me, (r, s, 1 - c, x))
        else:
            add(UPPER, me, (r, s, 0, c))
            add(LOWER, me, (r, s, 1, c))
        beside = (r, 1 - s, c, x)
        across = (r, s, 1 - c, x if c == 0 else 1 - x)
        turns = turns_at(rows, r, c, x)
        if inner(s, c) and turns:
            add(FIRST, across, me)
            add(OUT, across, me)
        elif inner(s, c):
            add(INTO, beside, me)
        elif not turns and beside != origin:
            add(OUT, beside, me)
        if inner(s, c) and me != origin:
            add(FIRST, me, beside)
        on = r + 1 if c == 0 else r - 1
        if 0 <= on < rows:
            to = (on, s, c, x)
            if me != origin:
                add(NEAR, me, to)
            if c != x:
                add(FAR, me, to)
            if inner(s, c) and not turns:
                add(LATE, me, to)
    for s in range(2):
        for x in range(2):
            add(NEAR, (rows - 1, s, 0, x), (rows - 1, 1 - s, 1, 1 - x))
        add(NEAR, (0, s, 1, 1), (0, 1 - s, 0, 1))
        add(BEND, (rows - 1, s, 0, 1), (rows - 1, 1 - s, 1, 0))
    add(NEAR, (0, 1, 1, 0), (0, 1, 0, 0))
    add(BEND, (0, 0, 1, 1), (0, 1, 0, 1))
    for source, (r, s, c, x) in spun(rows):
        add(TURN, source, (r, s, c, x))
        add(OTHER + TURN, (r, s, c, x), (r, s, 1 - c, x))
    add(NEAR, (0, 0, 1, 0), (1, 0, 0, 0))
    add(FIRST, (0, 0, 1, 0), (0, 1, 0, 0))
    for move in MOVES:
        way[HOME + move] = back(way[move])
    way[HOME + TAIL] = []
    for move, source, target in ((TURN, origin, (0, 0, 0, 1)), (FIRST, (1, 0, 1, 0), origin)):
        add(move, source, target)
        add(HOME + TAIL, target, source)
    return way


def back(pairs):
    return [(b, a) for a, b in pairs]


def count_terms(count_tile):
    clamped = jnp.maximum(count_tile.astype(jnp.float32), 1.0)
    weight = 0.1 + 0.25 * jnp.sqrt(clamped)
    return jnp.where(count_tile > 0, weight, 0.0), jnp.log(clamped)


def residual_of(scores, weight, log_count):
    kept = weight * jnp.clip(scores - log_count, -clip_bound, clip_bound)
    return jnp.where(weight > 0.0, kept, 0.25 + 0.25 * jnp.tanh(0.5 * scores))


def terms_kernel(first, counts, weights, logs, token, tile, sems):
    rounds = weights.shape[0]

    def fetch(k):
        return pltpu.make_async_copy(counts.at[2 * k + first[0]], tile.at[k], sems.at[k])

    for k in range(rounds):
        fetch(k).start()
    for k in range(rounds):
        fetch(k).wait()
        weights[k], logs[k] = count_terms(tile[k])
    token[...] = jnp.zeros_like(token)


def prepare(counts, first):
    rounds, size, _ = counts.shape
    shape = pltpu.VMEM((rounds // 2, size, size), jnp.float32)
    hbm = pl.BlockSpec(memory_space=pltpu.HBM)
    vmem = pl.BlockSpec(memory_space=pltpu.VMEM)
    return pl.pallas_call(
        terms_kernel,
        out_shape=[shape, shape, jax.ShapeDtypeStruct((8, 128), jnp.int32)],
        in_specs=[pl.BlockSpec(memory_space=pltpu.SMEM), hbm],
        out_specs=[vmem] * 3,
        scratch_shapes=[
            pltpu.VMEM((rounds // 2, size, size), jnp.int32),
            pltpu.SemaphoreType.DMA((rounds // 2,)),
        ],
        compiler_params=pltpu.CompilerParams(vmem_limit_bytes=2 * rounds * size * size + (4 << 20)),
        cost_estimate=pl.CostEstimate(
            flops=20 * rounds * size * size, bytes_accessed=6 * rounds * size * size, transcendentals=rounds * size * size
        ),
    )(first, counts)


def split(value):
    high = value.astype(jnp.bfloat16)
    return high, (value - high.astype(jnp.float32)).astype(jnp.bfloat16)


def dot(left, right, dims):
    return lax.dot_general(left, right, (dims, ((), ())), preferred_element_type=jnp.float32)


ACTIVE, MAIN, PARTNER, TILE, SWAP, CORE, OUT_MAIN, OUT_OTHER, ZERO = range(9)
LINES = ((0,), (1,), (2,), (3, 4))
BLOCKS = (
    (KEEP, OTHER + KEEP),
    (KEEP, FIRST, NEAR, TURN, OTHER + KEEP, OTHER + FIRST, OTHER + NEAR),
    (KEEP, FIRST, INTO, NEAR, TURN, OTHER + KEEP, OTHER + FIRST, OTHER + INTO),
    (KEEP, LATE, OUT, TURN, FAR, BEND, OTHER + NEAR, OTHER + FIRST, OTHER + OUT, OTHER + LATE, OTHER + TURN),
)
OUTS = (
    (0, CROSS + 0),
    (0, CROSS + 0, 1, 2, CROSS + 1, CROSS + 2),
    (CROSS + 0, 1, 2, CROSS + 1),
    (CROSS + 2, 3, 4, CROSS + 3),
)


def plan(players):
    chips = players // 2
    table = np.zeros((players, 2, 5, 9), np.int32)
    for player in range(players):
        for x in range(2):
            chip, c = player // 2, player % 2
            native, within = c == x, inner(chip % 2, c)
            rows = chips // 2
            spun_to = [target for _, target in spun(rows)]

            def sources(core):
                me = (chip // 2, chip % 2, core, x)
                within, turns = inner(chip % 2, core), turns_at(rows, chip // 2, core, x)
                one = INTO if within and not turns else FIRST
                two = FIRST if me == (0, 0, 0, 0) else NEAR
                three = TURN if me in spun_to else LATE if within and not turns else OUT
                return {0: KEEP, 1: one, 2: two, 3: three, 4: BEND if turns else FAR}

            main = sources(c)
            other = {k: OTHER + move for k, move in sources(1 - c).items()}
            if native:
                turns = [(0, 0), (1, 2), (2, 1), (3, 3), None]
            elif within:
                turns = [None, (1, 1), (2, 0), (3, 2), (3, 3)]
            else:
                turns = [None, (1, 0), (2, 1), (3, 2), (3, 3)]
            for line, turn in enumerate(turns):
                stage = min(line, 3)
                row = table[player, x, line]
                row[:] = -1
                row[ACTIVE] = turn is not None
                row[CORE] = c
                if turn is not None:
                    k = turn[1]
                    ahead = k if native else k + 1
                    ahead_low = ahead if c == 1 else k
                    turned = chip + ahead_low >= chips
                    source, partner, out = main[ahead], other[k], CROSS + k
                    if player == 0:
                        source = KEEP if x == 0 else TURN
                        turned = x == 1
                    if player == 1 and x == 0 and k == 0:
                        partner, out = KEEP, 0
                    row[MAIN] = BLOCKS[stage].index(source)
                    row[PARTNER] = BLOCKS[stage].index(partner)
                    row[TILE] = k
                    row[SWAP] = turned
                    row[OUT_MAIN] = OUTS[stage].index(ahead)
                    row[OUT_OTHER] = OUTS[stage].index(out)
                elif stage == 0:
                    row[ZERO] = OUTS[stage].index(CROSS if player == 1 and x == 0 else 0)
                else:
                    row[ZERO] = OUTS[stage].index(4)
    return table


def meet_kernel(lines, n_blocks, n_out, n_kept, mains, partners, cfg, weights, logs, *refs):
    blocks = refs[:n_blocks]
    outs = refs[n_blocks + n_kept : n_blocks + n_kept + n_out]
    high, low, res_high, res_low, grad = refs[n_blocks + n_kept + n_out :]
    half = grad.shape[1] // 2
    size = weights.shape[1]
    pad = high.shape[2]
    if pad > half:
        rest = jnp.zeros((2, 2, pad - (half - half % 16), size), jnp.bfloat16)
        high[:, :, half - half % 16 : pad, :] = rest
        low[:, :, half - half % 16 : pad, :] = rest

    for q in lines:

        @pl.when(cfg[0, 9 * q + ACTIVE] == 1)
        def _():
            core = cfg[0, 9 * q + CORE]
            swap = cfg[0, 9 * q + SWAP]
            for which, column, candidates in ((0, MAIN, mains), (1, PARTNER, partners)):
                for b in candidates:

                    @pl.when(cfg[0, 9 * q + column] == b)
                    def _():
                        for h in range(2):
                            to = h if which == 0 else jnp.where(swap == 1, 1 - h, h)
                            hi, lo = split(blocks[b][h * half : (h + 1) * half, :])
                            high[which, to, 0:half, :] = hi
                            low[which, to, 0:half, :] = lo

            tile = cfg[0, 9 * q + TILE]
            up_h = high[core].reshape(2 * pad, size)
            up_l = low[core].reshape(2 * pad, size)
            lo_h = high[1 - core].reshape(2 * pad, size)
            lo_l = low[1 - core].reshape(2 * pad, size)
            right = jnp.concatenate([lo_h, lo_l, lo_h], axis=0)
            left = jnp.concatenate([up_h, up_h, up_l], axis=0)
            rows = min(size, 256)
            for s in range(size // rows):
                band = slice(s * rows, (s + 1) * rows)
                scores = dot(left[:, band], right, ((0,), (0,)))
                hi, lo = split(residual_of(scores, weights[tile, band, :], logs[tile, band, :]))
                res_high[band, :] = hi
                res_low[band, :] = lo
            rh = res_high[...]
            rl = res_low[...]
            across = ((1,), (1,))
            along = ((1,), (0,))
            grad_upper = dot(lo_h, rh, across) + dot(lo_l, rh, across) + dot(lo_h, rl, across)
            grad_lower = dot(up_h, rh, along) + dot(up_l, rh, along) + dot(up_h, rl, along)
            for h in range(2):
                band = slice(h * pad, h * pad + half)
                for which, value in ((0, grad_upper), (1, grad_lower)):
                    target = jnp.where(core == 0, which, 1 - which)
                    to = jnp.where((swap == 1) & (target == 1), 1 - h, h)
                    grad[target, pl.ds(pl.multiple_of(to * half, 8), half), :] = value[band, :]
            for o in range(n_out):
                for which, column in ((0, OUT_MAIN), (1, OUT_OTHER)):

                    @pl.when(cfg[0, 9 * q + column] == o)
                    def _():
                        outs[o][...] = grad[which]

        for o in range(n_out):

            @pl.when(cfg[0, 9 * q + ZERO] == o)
            def _():
                outs[o][...] = jnp.zeros(grad.shape[1:], jnp.float32)


def vmem_budget(double, size):
    return 24 * double * size + 16 * size * size + (1 << 20)


def meet(stage, cfg, terms, blocks, slots):
    lines = LINES[stage]
    meetings = len(lines)
    names = BLOCKS[stage]
    mains = [i for i, name in enumerate(names) if name < OTHER]
    partners = [i for i, name in enumerate(names) if name >= OTHER or name == KEEP]
    blocks = [pltpu.with_memory_space_constraint(blocks[name], pltpu.VMEM) for name in names]
    kept = [pltpu.with_memory_space_constraint(slots[name], pltpu.VMEM) for name in OUTS[stage] if name in slots]
    fresh = len(OUTS[stage]) - len(kept)
    double, size = blocks[0].shape
    half = double // 2
    pad = -(-half // 16) * 16
    n_out = len(kept) + fresh
    shape = pltpu.VMEM(blocks[0].shape, jnp.float32)
    vmem = pl.BlockSpec(memory_space=pltpu.VMEM)
    call = pl.pallas_call(
        functools.partial(meet_kernel, lines, len(blocks), n_out, len(kept), mains, partners),
        out_shape=[shape] * n_out,
        in_specs=[pl.BlockSpec(memory_space=pltpu.SMEM)]
        + [vmem] * (2 + len(blocks) + len(kept)),
        out_specs=[vmem] * n_out,
        input_output_aliases={3 + len(blocks) + i: i for i in range(len(kept))},
        scratch_shapes=[
            pltpu.VMEM((2, 2, pad, size), jnp.bfloat16),
            pltpu.VMEM((2, 2, pad, size), jnp.bfloat16),
            pltpu.VMEM((size, size), jnp.bfloat16),
            pltpu.VMEM((size, size), jnp.bfloat16),
            pltpu.VMEM((2, double, size), jnp.float32),
        ],
        compiler_params=pltpu.CompilerParams(vmem_limit_bytes=vmem_budget(double, size)),
        cost_estimate=pl.CostEstimate(
            flops=meetings * 18 * half * 2 * size * size,
            bytes_accessed=meetings * (4 * size * size + 32 * half * size),
            transcendentals=meetings * 3 * size * size,
        ),
    )
    results = call(cfg, *terms, *blocks, *kept)
    return {**slots, **dict(zip(OUTS[stage], results))}


def play(factors, state, counts):
    players = lax.axis_size("blk")
    chips = players // 2
    way = routes(chips // 2)

    def send(block, move):
        return lax.ppermute(block, AXES, way[move])

    player = lax.axis_index("blk")
    x = lax.axis_index("rep")
    c = player % 2
    pick = jnp.where
    index = (2 * player + x).astype(jnp.uint32)
    parity = pick(c == x, 0, 1)
    scalars = (index, parity, player == 0, c == x, c == 0, x == 0)
    factors, (index, parity, leader, native, core_0, plane_0) = lax.optimization_barrier((factors, scalars))

    features, _ = factors.shape[2:]
    half = -(-features // 8) * 8
    rest = ((0, half - features), (0, 0))
    upper, lower = jnp.pad(factors[0, 0], rest), jnp.pad(factors[0, 1], rest)
    kept = send(pick(core_0, lower, upper), KEEP)
    far_upper = send(upper, UPPER)
    far_lower = send(lower, LOWER)
    table = plan(players)
    zero = jnp.uint32(0)
    cfg = lax.dynamic_slice(
        jnp.asarray(table.reshape(2 * players, -1)), (index, zero), (1, table[0, 0].size)
    )
    weights, logs, token = prepare(pltpu.with_memory_space_constraint(counts[0], pltpu.HBM), parity[None])
    kept, far_upper, far_lower, token = lax.optimization_barrier((kept, far_upper, far_lower, token))
    cfg = cfg + token[0, 0]
    terms = [pltpu.with_memory_space_constraint(term, pltpu.VMEM) for term in (weights, logs)]
    got = {}
    slots = {}
    got[KEEP] = jnp.concatenate(
        [pick(native, pick(core_0, upper, lower), kept), pick(core_0, far_upper, far_lower)]
    )

    main0 = got[KEEP]
    got[FIRST] = send(main0, FIRST)
    main2 = got[NEAR] = send(main0, NEAR)
    got[TURN] = send(main0, TURN)
    got[OTHER + KEEP] = send(main0, CORES)
    slots = meet(0, cfg, terms, got, slots)
    got[INTO] = send(main2, INTO)
    got[FAR] = send(main2, FAR)
    got[OTHER + NEAR] = send(main2, CORES)
    got[OTHER + FIRST] = send(got[FIRST], CORES)
    got[OTHER + TURN] = send(got[TURN], OTHER + TURN)
    slots = meet(1, cfg, terms, got, slots)
    got[LATE] = send(got[INTO], LATE)
    got[OUT] = send(main2, OUT)
    got[BEND] = send(main2, BEND)
    got[OTHER + INTO] = send(got[INTO], CORES)
    slots = meet(2, cfg, terms, got, slots)
    got[OTHER + OUT] = send(got[OUT], CORES)
    got[OTHER + LATE] = send(got[LATE], CORES)

    def own(grad):
        return pick(leader, 0.0, grad)

    near0 = send(slots[CROSS + 0], CORES)
    sum1 = own(slots[1]) + send(slots[CROSS + 1], CORES)
    sum1, got[OTHER + OUT] = lax.optimization_barrier((sum1, got[OTHER + OUT]))
    from_first = send(sum1, HOME + FIRST)
    slots = meet(3, cfg, terms, got, slots)
    sum3 = own(slots[3]) + send(slots[CROSS + 3], CORES)
    from_late = send(sum3, HOME + LATE)
    from_out = send(sum3, HOME + OUT)
    from_turn = send(sum3, HOME + TURN)
    sum2 = own(slots[2]) + send(slots[CROSS + 2], CORES)
    lead = pick(plane_0, slots[0], slots[4]) + slots[1] + slots[2] + slots[3]
    tail = send(pick(plane_0, sum2, lead), HOME + TAIL)
    grad4 = own(slots[4])
    from_far = send(grad4, HOME + FAR)
    from_bend = send(grad4, HOME + BEND)
    from_into = send(sum1 + from_late, HOME + INTO)
    sum2 = sum2 + from_out + from_into + from_far + from_bend
    from_near = send(sum2, HOME + NEAR)
    mine = pick(leader, pick(plane_0, lead, 0.0), slots[0]) + near0 + from_first + from_turn
    sum0 = mine + from_near + tail
    here, there = sum0[:half], sum0[half:]
    kept = send(here, HOME + KEEP)
    far_upper = send(there, HOME + UPPER)
    far_lower = send(there, HOME + LOWER)
    upper = pick(native, pick(core_0, here, kept), far_upper)
    lower = pick(native, pick(core_0, kept, here), far_lower)
    total = jnp.stack([upper[:features], lower[:features]], axis=1)
    new_state = state[0].transpose(1, 0, 2) + total * total
    step = total / jnp.sqrt(new_state)
    return (step.transpose(1, 0, 2)[None], new_state.transpose(1, 0, 2)[None])


def solution(mesh):
    in_specs = (
        P("blk", None, "rep", None),
        P("blk", None, "rep", None),
        P("blk", None, None, None),
    )
    out_specs = (P("blk", None, "rep", None), P("blk", None, "rep", None))
    return jax.shard_map(play, mesh=mesh, in_specs=in_specs, out_specs=out_specs, check_vma=False)
```

```python
import functools
import jax
import jax.numpy as jnp
import numpy as np
from jax import lax
from jax.experimental import pallas as pl
from jax.experimental.layout import Layout, with_layout_constraint
from jax.experimental.pallas import tpu as pltpu
from jax.sharding import PartitionSpec as P


clip_bound = 2.0
AXES = ("blk", "rep")

MOVES = range(12)
KEEP, UPPER, LOWER, CORES, FIRST, NEAR, INTO, OUT, FAR, BEND, LATE, TURN = MOVES
TAIL = 12
HOME, OTHER = 100, 200
CROSS = 10


def place(row, side, core, plane):
    return ((2 * row + side) * 2 + core) * 2 + plane


def inner(side, core):
    return core == side


def turns_at(rows, row, core, plane):
    return row == rows - 1 and core == 1 or row == 0 and core == 0 and plane == 1


def spun(rows):
    pairs = [((0, 1, 1, 1), (0, 1, 0, 1)), ((0, 0, 1, 1), (1, 0, 0, 1))]
    pairs.append(((1, 0, 1, 0), (0, 1, 0, 0)))
    for x in range(2):
        pairs.append(((rows - 1, 0, 0, 1 - x), (rows - 1, 0, 1, x)))
        pairs.append(((rows - 1, 1, 0, 1 - x), (rows - 2, 1, 1, x)))
    return pairs


def routes(rows):
    every = [(r, s, c, x) for r in range(rows) for s in range(2) for c in range(2) for x in range(2)]
    way = {move: [] for move in (*MOVES, OTHER + TURN)}
    origin = (0, 0, 0, 0)

    def add(move, source, target):
        way[move].append((place(*source), place(*target)))

    for me in every:
        r, s, c, x = me
        add(CORES, me, (r, s, 1 - c, x))
        if c == x:
            add(KEEP, me, (r, s, 1 - c, x))
        else:
            add(UPPER, me, (r, s, 0, c))
            add(LOWER, me, (r, s, 1, c))
        beside = (r, 1 - s, c, x)
        across = (r, s, 1 - c, x if c == 0 else 1 - x)
        turns = turns_at(rows, r, c, x)
        if inner(s, c) and turns:
            add(FIRST, across, me)
            add(OUT, across, me)
        elif inner(s, c):
            add(INTO, beside, me)
        elif not turns and beside != origin:
            add(OUT, beside, me)
        if inner(s, c) and me != origin:
            add(FIRST, me, beside)
        on = r + 1 if c == 0 else r - 1
        if 0 <= on < rows:
            to = (on, s, c, x)
            if me != origin:
                add(NEAR, me, to)
            if c != x:
                add(FAR, me, to)
            if inner(s, c) and not turns:
                add(LATE, me, to)
    for s in range(2):
        for x in range(2):
            add(NEAR, (rows - 1, s, 0, x), (rows - 1, 1 - s, 1, 1 - x))
        add(NEAR, (0, s, 1, 1), (0, 1 - s, 0, 1))
        add(BEND, (rows - 1, s, 0, 1), (rows - 1, 1 - s, 1, 0))
    add(NEAR, (0, 1, 1, 0), (0, 1, 0, 0))
    add(BEND, (0, 0, 1, 1), (0, 1, 0, 1))
    for source, (r, s, c, x) in spun(rows):
        add(TURN, source, (r, s, c, x))
        add(OTHER + TURN, (r, s, c, x), (r, s, 1 - c, x))
    add(NEAR, (0, 0, 1, 0), (1, 0, 0, 0))
    add(FIRST, (0, 0, 1, 0), (0, 1, 0, 0))
    for move in MOVES:
        way[HOME + move] = back(way[move])
    add(TURN, origin, (0, 0, 0, 1))
    way[HOME + TAIL] = back(way[TURN][-1:])
    return way


def back(pairs):
    return [(b, a) for a, b in pairs]


def count_terms(count_tile):
    clamped = jnp.maximum(count_tile.astype(jnp.float32), 1.0)
    weight = 0.1 + 0.25 * jnp.sqrt(clamped)
    return jnp.where(count_tile > 0, weight, 0.0), jnp.log(clamped)


def residual_of(scores, weight, log_count):
    kept = weight * jnp.clip(scores - log_count, -clip_bound, clip_bound)
    return jnp.where(weight > 0.0, kept, 0.25 + 0.25 * jnp.tanh(0.5 * scores))


def terms_kernel(first, counts, weights, logs, token, tile, sems):
    rounds = weights.shape[0]

    def fetch(k):
        return pltpu.make_async_copy(counts.at[2 * k + first[0]], tile.at[k], sems.at[k])

    for k in range(rounds):
        fetch(k).start()
    for k in range(rounds):
        fetch(k).wait()
        weights[k], logs[k] = count_terms(tile[k])
    token[...] = jnp.zeros_like(token)


def prepare(counts, first):
    rounds, size, _ = counts.shape
    shape = pltpu.VMEM((rounds // 2, size, size), jnp.float32)
    hbm = pl.BlockSpec(memory_space=pltpu.HBM)
    vmem = pl.BlockSpec(memory_space=pltpu.VMEM)
    return pl.pallas_call(
        terms_kernel,
        out_shape=[shape, shape, jax.ShapeDtypeStruct((8, 128), jnp.int32)],
        in_specs=[pl.BlockSpec(memory_space=pltpu.SMEM), hbm],
        out_specs=[vmem] * 3,
        scratch_shapes=[
            pltpu.VMEM((rounds // 2, size, size), jnp.int32),
            pltpu.SemaphoreType.DMA((rounds // 2,)),
        ],
        compiler_params=pltpu.CompilerParams(vmem_limit_bytes=2 * rounds * size * size + (4 << 20)),
        cost_estimate=pl.CostEstimate(
            flops=20 * rounds * size * size, bytes_accessed=6 * rounds * size * size, transcendentals=rounds * size * size
        ),
    )(first, counts)


def split(value):
    high = value.astype(jnp.bfloat16)
    return high, (value - high.astype(jnp.float32)).astype(jnp.bfloat16)


def dot(left, right, dims):
    return lax.dot_general(left, right, (dims, ((), ())), preferred_element_type=jnp.float32)


ACTIVE, MAIN, PARTNER, TILE, SWAP, CORE, OUT_MAIN, OUT_OTHER, ZERO = range(9)
LINES = ((0,), (1,), (2,), (3, 4))
BLOCKS = (
    (KEEP, OTHER + KEEP),
    (KEEP, FIRST, NEAR, TURN, OTHER + KEEP, OTHER + FIRST, OTHER + NEAR),
    (KEEP, FIRST, INTO, NEAR, TURN, OTHER + KEEP, OTHER + FIRST, OTHER + INTO),
    (KEEP, NEAR, LATE, OUT, TURN, FAR, BEND, OTHER + NEAR, OTHER + OUT, OTHER + LATE, OTHER + TURN),
)
OUTS = (
    (0, CROSS + 0),
    (0, CROSS + 0, 1, 2, CROSS + 1, CROSS + 2),
    (CROSS + 0, 1, 2, CROSS + 1),
    (CROSS + 2, 3, 4, CROSS + 3),
)


def plan(players):
    chips = players // 2
    table = np.zeros((players, 2, 5, 9), np.int32)
    for player in range(players):
        for x in range(2):
            chip, c = player // 2, player % 2
            native, within = c == x, inner(chip % 2, c)
            rows = chips // 2
            spun_to = [target for _, target in spun(rows)]

            def sources(core):
                me = (chip // 2, chip % 2, core, x)
                within, turns = inner(chip % 2, core), turns_at(rows, chip // 2, core, x)
                one = INTO if within and not turns else FIRST
                three = TURN if me in spun_to else LATE if within and not turns else OUT
                return {0: KEEP, 1: one, 2: NEAR, 3: three, 4: BEND if turns else FAR}

            main = sources(c)
            other = {k: OTHER + move for k, move in sources(1 - c).items()}
            if native:
                turns = [(0, 0), (1, 2), (2, 1), (3, 3), None]
            elif within:
                turns = [None, (1, 1), (2, 0), (3, 2), (3, 3)]
            else:
                turns = [None, (1, 0), (2, 1), (3, 2), (3, 3)]
            for line, turn in enumerate(turns):
                stage = min(line, 3)
                row = table[player, x, line]
                row[:] = -1
                row[ACTIVE] = turn is not None
                row[CORE] = c
                if turn is not None:
                    k = turn[1]
                    ahead = k if native else k + 1
                    ahead_low = ahead if c == 1 else k
                    turned = chip + ahead_low >= chips
                    source, partner, out = main[ahead], other[k], CROSS + k
                    if player == 0:
                        source = KEEP if x == 0 else TURN
                        turned = x == 1
                    if player == 1 and x == 0 and k == 0:
                        partner, out = KEEP, 0
                    elif player == 1 and x == 0 and k >= 2:
                        partner = main[k]
                    row[MAIN] = BLOCKS[stage].index(source)
                    row[PARTNER] = BLOCKS[stage].index(partner)
                    row[TILE] = k
                    row[SWAP] = turned
                    row[OUT_MAIN] = OUTS[stage].index(ahead)
                    row[OUT_OTHER] = OUTS[stage].index(out)
                elif stage == 0:
                    row[ZERO] = OUTS[stage].index(CROSS if player == 1 and x == 0 else 0)
                else:
                    row[ZERO] = OUTS[stage].index(4)
    return table


def meet_kernel(lines, n_blocks, n_out, n_kept, mains, partners, cfg, weights, logs, *refs):
    blocks = refs[:n_blocks]
    outs = refs[n_blocks + n_kept : n_blocks + n_kept + n_out]
    high, low, res_high, res_low, grad = refs[n_blocks + n_kept + n_out :]
    half = grad.shape[1] // 2
    size = weights.shape[1]
    pad = high.shape[2]
    if pad > half:
        rest = jnp.zeros((2, 2, pad - (half - half % 16), size), jnp.bfloat16)
        high[:, :, half - half % 16 : pad, :] = rest
        low[:, :, half - half % 16 : pad, :] = rest

    for q in lines:

        @pl.when(cfg[0, 9 * q + ACTIVE] == 1)
        def _():
            core = cfg[0, 9 * q + CORE]
            swap = cfg[0, 9 * q + SWAP]
            for which, column, candidates in ((0, MAIN, mains), (1, PARTNER, partners)):
                for b in candidates:

                    @pl.when(cfg[0, 9 * q + column] == b)
                    def _():
                        for h in range(2):
                            to = h if which == 0 else jnp.where(swap == 1, 1 - h, h)
                            hi, lo = split(blocks[b][h * half : (h + 1) * half, :])
                            high[which, to, 0:half, :] = hi
                            low[which, to, 0:half, :] = lo

            tile = cfg[0, 9 * q + TILE]
            up_h = high[core].reshape(2 * pad, size)
            up_l = low[core].reshape(2 * pad, size)
            lo_h = high[1 - core].reshape(2 * pad, size)
            lo_l = low[1 - core].reshape(2 * pad, size)
            right = jnp.concatenate([lo_h, lo_l, lo_h], axis=0)
            left = jnp.concatenate([up_h, up_h, up_l], axis=0)
            rows = min(size, 256)
            for s in range(size // rows):
                band = slice(s * rows, (s + 1) * rows)
                scores = dot(left[:, band], right, ((0,), (0,)))
                hi, lo = split(residual_of(scores, weights[tile, band, :], logs[tile, band, :]))
                res_high[band, :] = hi
                res_low[band, :] = lo
            rh = res_high[...]
            rl = res_low[...]
            across = ((1,), (1,))
            along = ((1,), (0,))
            grad_upper = dot(lo_h, rh, across) + dot(lo_l, rh, across) + dot(lo_h, rl, across)
            grad_lower = dot(up_h, rh, along) + dot(up_l, rh, along) + dot(up_h, rl, along)
            for h in range(2):
                band = slice(h * pad, h * pad + half)
                for which, value in ((0, grad_upper), (1, grad_lower)):
                    target = jnp.where(core == 0, which, 1 - which)
                    to = jnp.where((swap == 1) & (target == 1), 1 - h, h)
                    grad[target, pl.ds(pl.multiple_of(to * half, 8), half), :] = value[band, :]
            for o in range(n_out):
                for which, column in ((0, OUT_MAIN), (1, OUT_OTHER)):

                    @pl.when(cfg[0, 9 * q + column] == o)
                    def _():
                        outs[o][...] = grad[which]

        for o in range(n_out):

            @pl.when(cfg[0, 9 * q + ZERO] == o)
            def _():
                outs[o][...] = jnp.zeros(grad.shape[1:], jnp.float32)


def vmem_budget(double, size):
    return 24 * double * size + 16 * size * size + (1 << 20)


def meet(stage, table, cfg, terms, blocks, slots):
    lines = LINES[stage]
    meetings = len(lines)
    names = BLOCKS[stage]
    mains, partners = ({int(i) for i in np.unique(table[:, :, lines, column])} - {-1} for column in (MAIN, PARTNER))
    blocks = [pltpu.with_memory_space_constraint(blocks[name], pltpu.VMEM) for name in names]
    kept = [pltpu.with_memory_space_constraint(slots[name], pltpu.VMEM) for name in OUTS[stage] if name in slots]
    fresh = len(OUTS[stage]) - len(kept)
    double, size = blocks[0].shape
    half = double // 2
    pad = -(-half // 16) * 16
    n_out = len(kept) + fresh
    shape = pltpu.VMEM(blocks[0].shape, jnp.float32)
    vmem = pl.BlockSpec(memory_space=pltpu.VMEM)
    call = pl.pallas_call(
        functools.partial(meet_kernel, lines, len(blocks), n_out, len(kept), mains, partners),
        out_shape=[shape] * n_out,
        in_specs=[pl.BlockSpec(memory_space=pltpu.SMEM)]
        + [vmem] * (2 + len(blocks) + len(kept)),
        out_specs=[vmem] * n_out,
        input_output_aliases={3 + len(blocks) + i: i for i in range(len(kept))},
        scratch_shapes=[
            pltpu.VMEM((2, 2, pad, size), jnp.bfloat16),
            pltpu.VMEM((2, 2, pad, size), jnp.bfloat16),
            pltpu.VMEM((size, size), jnp.bfloat16),
            pltpu.VMEM((size, size), jnp.bfloat16),
            pltpu.VMEM((2, double, size), jnp.float32),
        ],
        compiler_params=pltpu.CompilerParams(vmem_limit_bytes=vmem_budget(double, size)),
        cost_estimate=pl.CostEstimate(
            flops=meetings * 18 * half * 2 * size * size,
            bytes_accessed=meetings * (4 * size * size + 32 * half * size),
            transcendentals=meetings * 3 * size * size,
        ),
    )
    results = call(cfg, *terms, *blocks, *kept)
    return {**slots, **dict(zip(OUTS[stage], results))}


def play(factors, state, counts):
    players = lax.axis_size("blk")
    chips = players // 2
    way = routes(chips // 2)

    def send(block, move):
        return lax.ppermute(block, AXES, way[move])

    player = lax.axis_index("blk")
    x = lax.axis_index("rep")
    c = player % 2
    pick = jnp.where
    index = (2 * player + x).astype(jnp.uint32)
    parity = pick(c == x, 0, 1)
    second = (player == 1) & (x == 0)
    scalars = (index, parity, player == 0, second, c == x, c == 0, x == 0)
    factors, (index, parity, leader, second, native, core_0, plane_0) = lax.optimization_barrier((factors, scalars))

    features, _ = factors.shape[2:]
    half = -(-features // 8) * 8
    rest = ((0, half - features), (0, 0))
    upper, lower = jnp.pad(factors[0, 0], rest), jnp.pad(factors[0, 1], rest)
    kept = send(pick(core_0, lower, upper), KEEP)
    far_upper = send(upper, UPPER)
    far_lower = send(lower, LOWER)
    table = plan(players)
    zero = jnp.uint32(0)
    cfg = lax.dynamic_slice(
        jnp.asarray(table.reshape(2 * players, -1)), (index, zero), (1, table[0, 0].size)
    )
    weights, logs, token = prepare(pltpu.with_memory_space_constraint(counts[0], pltpu.HBM), parity[None])
    cfg = cfg + token[0, 0]
    kept, far_upper, far_lower, cfg = lax.optimization_barrier((kept, far_upper, far_lower, cfg))
    terms = [pltpu.with_memory_space_constraint(term, pltpu.VMEM) for term in (weights, logs)]
    got = {}
    slots = {}
    got[KEEP] = jnp.concatenate(
        [pick(native, pick(core_0, upper, lower), kept), pick(core_0, far_upper, far_lower)]
    )

    main0 = got[KEEP]
    got[FIRST] = send(main0, FIRST)
    main2 = got[NEAR] = send(main0, NEAR)
    got[TURN] = send(main0, TURN)
    got[OTHER + KEEP] = send(main0, CORES)
    slots = meet(0, table, cfg, terms, got, slots)
    got[INTO] = send(main2, INTO)
    got[FAR] = send(main2, FAR)
    got[OTHER + NEAR] = send(main2, CORES)
    got[OTHER + FIRST] = send(got[FIRST], CORES)
    got[OTHER + TURN] = send(got[TURN], OTHER + TURN)
    slots = meet(1, table, cfg, terms, got, slots)
    got[LATE] = send(got[INTO], LATE)
    got[OUT] = send(main2, OUT)
    got[BEND] = send(main2, BEND)
    got[OTHER + INTO] = send(got[INTO], CORES)
    slots = meet(2, table, cfg, terms, got, slots)
    got[OTHER + OUT] = send(got[OUT], CORES)
    got[OTHER + LATE] = send(got[LATE], CORES)

    def own(grad):
        return pick(leader, 0.0, grad)

    near0 = send(slots[CROSS + 0], CORES)
    sum1 = own(slots[1]) + send(slots[CROSS + 1], CORES)
    sum1, got[OTHER + OUT] = lax.optimization_barrier((sum1, got[OTHER + OUT]))
    from_first = send(sum1, HOME + FIRST)
    slots = meet(3, table, cfg, terms, got, slots)
    sum3 = own(slots[3]) + pick(second, slots[CROSS + 3], 0.0) + send(slots[CROSS + 3], CORES)
    from_late = send(sum3, HOME + LATE)
    from_out = send(sum3, HOME + OUT)
    from_turn = send(sum3, HOME + TURN)
    sum2 = own(slots[2]) + pick(second, slots[CROSS + 2], 0.0) + send(slots[CROSS + 2], CORES)
    lead = pick(plane_0, slots[0], slots[4]) + slots[1] + slots[2] + slots[3]
    tail = send(lead, HOME + TAIL)
    grad4 = own(slots[4])
    from_far = send(grad4, HOME + FAR)
    from_bend = send(grad4, HOME + BEND)
    from_into = send(sum1 + from_late, HOME + INTO)
    sum2 = sum2 + from_out + from_into + from_far + from_bend
    from_near = send(sum2, HOME + NEAR)
    mine = pick(leader, pick(plane_0, lead, 0.0), slots[0]) + near0 + from_first + from_turn
    sum0 = mine + from_near + tail
    here, there = sum0[:half], sum0[half:]
    kept = send(here, HOME + KEEP)
    far_upper = send(there, HOME + UPPER)
    far_lower = send(there, HOME + LOWER)
    upper = pick(native, pick(core_0, here, kept), far_upper)
    lower = pick(native, pick(core_0, kept, here), far_lower)
    total = jnp.stack([upper[:features], lower[:features]])[None]
    total = with_layout_constraint(total, Layout(major_to_minor=(0, 2, 1, 3)))
    new_state = state + total * total
    step = total / jnp.sqrt(new_state)
    return (step, new_state)


def solution(mesh):
    in_specs = (
        P("blk", None, "rep", None),
        P("blk", None, "rep", None),
        P("blk", None, None, None),
    )
    out_specs = (P("blk", None, "rep", None), P("blk", None, "rep", None))
    return jax.shard_map(play, mesh=mesh, in_specs=in_specs, out_specs=out_specs, check_vma=False)
```
